32 devices in a mesh: rows: 8 (over z, y), cols: 4 (over x, core).
Axes of the slice: x: 2, y: 2, z: 4, core: 2. Of those that a mesh axis runs over, the one named last changes fastest.
Arguments:
- samples: float32 [64, 32768], P('cols', 'rows')
- loadings: bfloat16 [256, 32768], P(None, 'rows')
- omega_tiles: float32 [320, 512, 512], P(('rows', 'cols')), may hold values from -0.18 to 0.18
- omega_diagonal: float32 [32768], P('rows'), may hold values from 0.5 to 2
- tile_rows: int32 [320], replicated, may hold values from 0 to 63, as said below
- tile_cols: int32 [320], replicated, may hold values from 0 to 63, as said below
Outputs:
- new_tiles: float32 [320, 512, 512], P(('rows', 'cols'))
- new_diagonal: float32 [32768], P('rows')
The draws below stay inside these ranges and needn't reach their ends.
Inputs may be any that keep to these rules, and one draw needn't show every extreme that they name: Slot s belongs to group g = s // 40; tile_rows[s] lies between g * 8 and g * 8 + 7. A block row may hold any number of tiles, none included. `tile_cols`: of the 40 tiles of one group, at most 10 have column blocks in any one group h (blocks h * 8 to h * 8 + 7), and in every group exactly 10 have column blocks in some one group.
All inputs are finite; a program needn't handle non-finite values.
Results may differ from the reference program's by a relative error of at most 0.0003.
Values sent between devices are 32-bit elements; how exact they have to be, the bound alone decides.
No kernel may reach another device: no remote copies, remote signals or barrier semaphores. Data moves between devices by JAX's collectives and lax.ppermute only.
A program may use at most 64 MiB of HBM per device.

```python
import math
import jax
import jax.numpy as jnp
from jax import lax

BS = 512
K = 256
BR_DEV = 8
P_SIZE = 32768
NS = 64
GROUP_TILES = 40
CAP = 10
TILES = 320
N_ROWS = 8


def factor_parts(key):
    base_key = jax.random.fold_in(key, 4242)
    key_load, key_score, key_noise = jax.random.split(base_key, 3)
    factor_load = (jax.random.normal(key_load, (K, P_SIZE), jnp.float32) * P_SIZE ** (-0.5)).astype(jnp.bfloat16)
    latent = jax.random.normal(key_score, (NS, K), jnp.float32) * (P_SIZE / K) ** 0.5
    noise = jax.random.normal(key_noise, (NS, P_SIZE), jnp.float32)
    data = jnp.dot(latent, factor_load.astype(jnp.float32), precision=lax.Precision.HIGHEST) + noise
    return (factor_load, data)


def draw_samples(key, part):
    return factor_parts(key)[1]


def draw_loadings(key, part):
    return factor_parts(key)[0]


def pattern(key):
    base_key = jax.random.fold_in(key, 777)

    def draw_group(group):
        group_key = jax.random.fold_in(base_key, group)
        key_rows, key_hot, key_order, key_shuffle, key_cols = jax.random.split(group_key, 5)
        local_rows = jax.random.randint(key_rows, (GROUP_TILES,), 0, BR_DEV)
        slot_group = jnp.arange(N_ROWS * CAP) // CAP
        within = jnp.arange(N_ROWS * CAP) % CAP
        hot_group = jax.random.randint(key_hot, (), 0, N_ROWS)
        order_keys = jax.random.permutation(key_order, N_ROWS * CAP) + CAP
        order_keys = jnp.where(slot_group == hot_group, within, order_keys)
        picked = slot_group[jnp.argsort(order_keys)[:GROUP_TILES]]
        shuffle = jax.random.permutation(key_shuffle, GROUP_TILES)
        groups = picked[shuffle]
        local_cols = jax.random.randint(key_cols, (GROUP_TILES,), 0, BR_DEV)
        return (group * BR_DEV + local_rows, groups * BR_DEV + local_cols)
    row_ids, col_ids = jax.vmap(draw_group)(jnp.arange(N_ROWS))
    return (row_ids.reshape(-1).astype(jnp.int32), col_ids.reshape(-1).astype(jnp.int32))


def draw_tile_rows(key, part):
    return pattern(key)[0]


def draw_tile_cols(key, part):
    return pattern(key)[1]


def block_levels(key, shape, shards, low, largest):
    def one(axis_at, parts):
        draws = jax.random.uniform(jax.random.fold_in(jax.random.fold_in(key, 6), axis_at), (parts,), jnp.float32, low / len(shards), largest / len(shards))
        return jnp.repeat(jnp.exp(draws), shape[axis_at] // parts).reshape((-1,) + (1,) * (len(shape) - axis_at - 1))

    factor_of = one(*shards[0])
    for cut in shards[1:]:
        factor_of = factor_of * one(*cut)
    return factor_of


def gaussian(key, dims, scale, reach, cuts=(), kind=jnp.bfloat16):
    entries = jax.random.normal(key, dims, jnp.float32) * scale
    if len(cuts) > 0:
        entries = block_levels(key, dims, cuts, -0.22, 0.18) * entries
    return jnp.clip(entries, min=-reach, max=reach).astype(kind)


def setup_inputs(seed: int = 0) -> dict:
    seeds = jax.random.split(jax.random.key(seed), 7)
    return {
        "samples": draw_samples(jax.random.fold_in(seeds[6], 71), 0),
        "loadings": draw_loadings(jax.random.fold_in(seeds[6], 71), 0),
        "omega_tiles": gaussian(seeds[2], (TILES, BS, BS), 0.03, 0.18, ((0, 32),), jnp.float32),
        "omega_diagonal": jnp.clip(jnp.exp(math.log(2.0) - 1.3862944 * jax.random.uniform(seeds[3], (P_SIZE,), jnp.float32) ** block_levels(seeds[3], (P_SIZE,), ((0, 8),), -0.2, 0.2)), 0.5, 2.0),
        "tile_rows": draw_tile_rows(jax.random.fold_in(seeds[6], 71), 0),
        "tile_cols": draw_tile_cols(jax.random.fold_in(seeds[6], 71), 0),
    }


step_size = 0.5
penalty = 0.02


def reference(samples, loadings, omega_tiles, omega_diagonal, tile_rows, tile_cols):
    highest = lax.Precision.HIGHEST
    factor_load = loadings.astype(jnp.float32)
    scores = jnp.dot(samples, factor_load.T, precision=highest, preferred_element_type=jnp.float32)
    residual = samples - jnp.dot(scores, factor_load, precision=highest, preferred_element_type=jnp.float32)
    diagonal_mask = jnp.eye(BS, dtype=bool)

    def apply_tile(running, tile_entry):
        tile_block, row_block, col_block = tile_entry
        keep_mask = jnp.where((row_block == col_block) & diagonal_mask, 0.0, 1.0)
        source = lax.dynamic_slice_in_dim(residual, (col_block * BS).astype(jnp.int32), BS, 1)
        product = jnp.dot(source, (tile_block * keep_mask).T, precision=highest, preferred_element_type=jnp.float32)
        row_start = (row_block * BS).astype(jnp.int32)
        current = lax.dynamic_slice_in_dim(running, row_start, BS, 1)
        return lax.dynamic_update_slice_in_dim(running, current + product, row_start, 1), None

    applied, _ = lax.scan(apply_tile, residual * omega_diagonal, (omega_tiles, tile_rows, tile_cols))

    def tile_step(tile_entry):
        tile_block, row_block, col_block = tile_entry
        keep_mask = jnp.where((row_block == col_block) & diagonal_mask, 0.0, 1.0)
        row_start = (row_block * BS).astype(jnp.int32)
        col_start = (col_block * BS).astype(jnp.int32)
        rows_applied = lax.dynamic_slice_in_dim(applied, row_start, BS, 1)
        rows_resid = lax.dynamic_slice_in_dim(residual, row_start, BS, 1)
        cols_applied = lax.dynamic_slice_in_dim(applied, col_start, BS, 1)
        cols_resid = lax.dynamic_slice_in_dim(residual, col_start, BS, 1)
        first_term = jnp.dot(rows_applied.T, cols_resid, precision=highest, preferred_element_type=jnp.float32)
        second = jnp.dot(rows_resid.T, cols_applied, precision=highest, preferred_element_type=jnp.float32)
        gradient = 0.5 * (first_term + second) / NS
        stepped = (tile_block - step_size * gradient) * keep_mask
        return jnp.sign(stepped) * jnp.maximum(jnp.abs(stepped) - step_size * penalty, 0.0)

    new_tiles = lax.map(tile_step, (omega_tiles, tile_rows, tile_cols))
    diag_stat = jnp.sum(applied * residual, axis=0) / NS
    new_diagonal = omega_diagonal - step_size * (diag_stat - 1.0 / omega_diagonal)
    return new_tiles, new_diagonal
```

```python
import functools

import jax
import jax.numpy as jnp
from jax import lax
from jax.experimental import pallas as pl
from jax.experimental.pallas import tpu as pltpu
from jax.sharding import Mesh
from jax.sharding import PartitionSpec as P

step_size = 0.5
penalty = 0.02

ROWS = ("a", "u", "v")
COLS = ("x", "k")
PLANE = ("u", "v", "x")


NT = (((1,), (1,)), ((), ()))
NN = (((1,), (0,)), ((), ()))
TN = (((0,), (0,)), ((), ()))


def dot(left, right, dims):
    return lax.dot_general(left, right, dims, preferred_element_type=jnp.float32)


def split(value, pieces):
    found = []
    for _ in range(pieces):
        piece = value.astype(jnp.bfloat16)
        found.append(piece)
        value = value - piece.astype(jnp.float32)
    return found


def score_kernel(samples, loadings, out, total):
    step = pl.program_id(0)

    found = dot(jnp.concatenate(split(samples[...], 3), 0), loadings[...], NT)
    total[...] = jnp.where(step == 0, 0.0, total[...]) + found

    @pl.when(step == pl.num_programs(0) - 1)
    def _():
        rows = samples.shape[0]
        value = (total[2 * rows :] + total[rows : 2 * rows]) + total[:rows]
        for copy in range(out.shape[0]):
            out[copy] = value


def residual_kernel(place, scores, samples, loadings, whole, first, second, pieces):
    rows = samples.shape[0]
    half = rows // 2

    @pl.when(pl.program_id(0) == 0)
    def _():
        value = scores[0]
        for source in range(1, scores.shape[0]):
            value = value + scores[source]
        pieces[...] = jnp.concatenate(split(value, 3), 0)

    fitted = dot(pieces[...], loadings[...], NN)
    value = samples[...] - ((fitted[2 * rows :] + fitted[rows : 2 * rows]) + fitted[:rows])
    low, high = value[:half], value[half:]
    upper = place[1] == 1
    near = jnp.where(upper, high, low)
    far = jnp.where(upper, low, high)
    whole[:half] = near
    whole[half:] = far
    first[...] = near
    second[...] = far


def gather_kernel(index, *refs):
    count = len(refs) - 3
    sources, out, held, sem = refs[:count], refs[count], refs[count + 1], refs[count + 2]
    copies = [
        pltpu.make_async_copy(source, held.at[at], sem.at[at]) for at, source in enumerate(sources)
    ]
    for copy in copies:
        copy.start()
    for copy in copies:
        copy.wait()
    slots, half, width = out.shape
    blocks = held.shape[2] // width

    def move(slot, carry):
        code = index[slot]
        start = pl.multiple_of((code % blocks) * width, width)
        out[slot] = held[code // blocks, :, pl.ds(start, width)]
        return carry

    lax.fori_loop(0, slots, move, 0, unroll=4)


def masked(tile, is_diag):
    size = tile.shape[0]
    row = lax.broadcasted_iota(jnp.int32, (size, size), 0)
    col = lax.broadcasted_iota(jnp.int32, (size, size), 1)
    return jnp.where((row == col) & (is_diag == 1), 0.0, tile)


def product_kernel(
    x_count, row_local, is_diag, place, routed, tiles, keep, give, total
):
    step = pl.program_id(0)

    @pl.when(step == 0)
    def _():
        total[...] = jnp.zeros_like(total)

    block = total.shape[2]
    samples = total.shape[1]
    source_hi, source_lo = split(routed[...].reshape(samples, block), 2)
    tile_hi, tile_lo = split(masked(tiles[0], is_diag[step]), 2)
    stacked = dot(jnp.concatenate([source_hi, source_lo], 0), tile_hi, NT)
    product = stacked[:samples] + (stacked[samples:] + dot(source_hi, tile_lo, NT))
    total[row_local[step]] += product

    @pl.when(step == pl.num_programs(0) - 1)
    def _():
        half = keep.shape[1] // 2
        for out, core in ((keep, place[4]), (give, 1 - place[4])):
            for dx in range(x_count):
                for du in range(2):
                    source = ((place[1] ^ du) * 2 + core) * x_count + (place[3] + dx) % x_count
                    start = pl.multiple_of(source * half, half)
                    for at in range(total.shape[0]):
                        out[dx, du * half : (du + 1) * half, at * block : (at + 1) * block] = total[
                            at, pl.ds(start, half), :
                        ]


def applied_kernel(count, *refs):
    keep, got, residual, diagonal = refs[:4]
    arrived = refs[4 : 4 + count]
    whole, first, second = refs[4 + count :]
    half = first.shape[0]
    value = keep[0] + got[0]
    for other in arrived:
        value = value + other[...]
    value = value + diagonal[...] * residual[...]
    whole[...] = value
    first[...] = value[:half]
    second[...] = value[half:]


def gradient_kernel(
    x_count, scale, row_local, is_diag, place, routed_resid, routed_applied, tiles, diagonal, *refs
):
    count = 2 * x_count
    resid_parts, applied_parts = refs[:count], refs[count : 2 * count]
    new_tiles, new_diagonal, rows_resid, rows_applied, sem = refs[2 * count :]
    step = pl.program_id(0)
    block = tiles.shape[2]
    samples = rows_resid.shape[0]

    @pl.when(step == 0)
    def _():
        half = resid_parts[0].shape[0] // 2
        copies = []
        for which, (parts, rows) in enumerate(
            ((resid_parts, rows_resid), (applied_parts, rows_applied))
        ):
            for dk in range(2):
                for dx in range(x_count):
                    for du in range(2):
                        at = dk * x_count + dx
                        target = ((place[1] ^ du) * 2 + (place[4] ^ dk)) * x_count + (
                            place[3] + x_count - dx
                        ) % x_count
                        start = pl.multiple_of(target * half, half)
                        copies.append(
                            pltpu.make_async_copy(
                                parts[at].at[du * half : (du + 1) * half],
                                rows.at[pl.ds(start, half)],
                                sem.at[which, at, du],
                            )
                        )
        for copy in copies:
            copy.start()
        for copy in copies:
            copy.wait()
        stat = jnp.sum(rows_applied[...] * rows_resid[...], axis=0, keepdims=True) / samples
        new_diagonal[...] = diagonal[...] - step_size * (stat - 1.0 / diagonal[...])

    start = pl.multiple_of(row_local[step] * block, block)
    left_hi, left_lo = split(
        jnp.concatenate(
            [rows_applied[:, pl.ds(start, block)], rows_resid[:, pl.ds(start, block)]], 0
        ),
        2,
    )
    right_hi, right_lo = split(
        jnp.concatenate(
            [
                routed_resid[...].reshape(samples, block),
                routed_applied[...].reshape(samples, block),
            ],
            0,
        ),
        2,
    )
    left = jnp.concatenate([left_hi, left_hi, left_lo], 0)
    right = jnp.concatenate([right_hi, right_lo, right_hi], 0)
    summed = dot(left, right, TN)
    stepped = masked(tiles[0] - step_size * (summed * scale), is_diag[step])
    bound = step_size * penalty
    new_tiles[0] = stepped - jnp.clip(stepped, -bound, bound)


def per_device(samples, loadings, omega_tiles, omega_diagonal, tile_rows, tile_cols):
    f32 = jnp.float32
    a_count, x_count = lax.axis_size("a"), lax.axis_size("x")
    row_count, col_count = 4 * a_count, 2 * x_count
    a, u, v, x, k = (lax.axis_index(name) for name in ROWS + COLS)
    my_row = (a * 2 + u) * 2 + v
    sample_dev, var_dev = samples.shape
    half = sample_dev // 2
    sample_all = sample_dev * col_count
    factors = loadings.shape[0]
    tile_dev, block_size = omega_tiles.shape[:2]
    blocks_dev = var_dev // block_size
    plane = 4 * x_count
    any_spec = pl.BlockSpec(memory_space=pl.ANY)
    vmem = pl.BlockSpec(memory_space=pltpu.VMEM)
    shape = lambda *dims: jax.ShapeDtypeStruct(dims, f32)

    place = jnp.stack([a, u, v, x, k]).astype(jnp.int32)
    my_tiles = (my_row * col_count + x * 2 + k) * tile_dev
    my_rows = lax.dynamic_slice_in_dim(tile_rows, my_tiles, tile_dev)
    my_cols = lax.dynamic_slice_in_dim(tile_cols, my_tiles, tile_dev)
    row_local = my_rows - my_row * blocks_dev
    is_diag = (my_rows == my_cols).astype(jnp.int32)
    wanted = tile_cols.reshape(a_count, 2, 2, x_count, 2, tile_dev)
    wanted = lax.dynamic_index_in_dim(wanted, a, 0, keepdims=False)
    wanted = lax.dynamic_index_in_dim(wanted, k, 3, keepdims=False).reshape(plane * tile_dev)
    group = wanted // blocks_dev
    slot_index = (
        (((a + a_count - group // 4) % a_count) * 2 + (((group // 2) % 2) ^ u)) * 2
        + ((group % 2) ^ k)
    ) * blocks_dev + wanted % blocks_dev

    def permute(value, names, target):
        sizes = [lax.axis_size(name) for name in names]

        def flat(coords):
            at = 0
            for coord, size in zip(coords, sizes):
                at = at * size + coord
            return at

        def coords_of(at):
            coords = []
            for size in reversed(sizes):
                coords.append(at % size)
                at //= size
            return tuple(reversed(coords))

        total = 1
        for size in sizes:
            total *= size
        return lax.ppermute(
            value, names, [(at, flat(target(*coords_of(at)))) for at in range(total)]
        )

    def swap_core(value):
        return permute(value, ("k",), lambda k: (1 - k,))

    def shift_x(value, dx):
        return permute(value, ("x",), lambda x: ((x + dx) % x_count,))

    chunks = 4
    width = var_dev // chunks
    score_copies = pl.pallas_call(
        score_kernel,
        out_shape=shape(row_count, sample_dev, factors),
        grid=(chunks,),
        in_specs=[
            pl.BlockSpec((sample_dev, width), lambda s: (0, s)),
            pl.BlockSpec((factors, width), lambda s: (0, s)),
        ],
        out_specs=pl.BlockSpec((row_count, sample_dev, factors), lambda s: (0, 0, 0)),
        scratch_shapes=[pltpu.VMEM((3 * sample_dev, factors), f32)],
        name="scores",
    )(samples, loadings)
    score_terms = lax.all_to_all(score_copies, ROWS, 0, 0, tiled=True)
    residual, resid_near, resid_far = pl.pallas_call(
        residual_kernel,
        out_shape=[shape(sample_dev, var_dev), shape(half, var_dev), shape(half, var_dev)],
        grid_spec=pltpu.PrefetchScalarGridSpec(
            num_scalar_prefetch=1,
            grid=(chunks,),
            in_specs=[
                pl.BlockSpec((row_count, sample_dev, factors), lambda s, p: (0, 0, 0)),
                pl.BlockSpec((sample_dev, width), lambda s, p: (0, s)),
                pl.BlockSpec((factors, width), lambda s, p: (0, s)),
            ],
            out_specs=[
                pl.BlockSpec((sample_dev, width), lambda s, p: (0, s)),
                pl.BlockSpec((half, width), lambda s, p: (0, s)),
                pl.BlockSpec((half, width), lambda s, p: (0, s)),
            ],
            scratch_shapes=[pltpu.VMEM((3 * sample_dev, factors), jnp.bfloat16)],
        ),
        name="residual",
    )(place, score_terms, samples, loadings)

    def route(near, far):
        held = []
        for da in range(a_count):
            for dz, part in enumerate((near, far)):
                held.append(
                    permute(
                        part,
                        ("a", "u", "v", "k"),
                        lambda a, u, v, k: ((a + da) % a_count, u ^ dz, k, v),
                    )
                )
        sources = []
        for part in held:
            sources += [part, swap_core(part)]
        slots = pl.pallas_call(
            gather_kernel,
            out_shape=shape(plane * tile_dev, half, block_size),
            grid_spec=pltpu.PrefetchScalarGridSpec(
                num_scalar_prefetch=1,
                grid=(1,),
                in_specs=[any_spec] * len(sources),
                out_specs=pl.BlockSpec(
                    (plane * tile_dev, half, block_size), lambda s, i: (0, 0, 0)
                ),
                scratch_shapes=[
                    pltpu.VMEM((len(sources), half, var_dev), f32),
                    pltpu.SemaphoreType.DMA((len(sources),)),
                ],
            ),
            name="gather_slots",
        )(slot_index, *sources)
        return lax.all_to_all(
            slots.reshape(plane, tile_dev, half, block_size), PLANE, 0, 0, tiled=True
        )

    def own_rows(whole):
        parts = [whole] + [shift_x(whole, dx) for dx in range(1, x_count)]
        return parts + [swap_core(part) for part in parts]

    routed_resid = route(resid_near, resid_far)
    resid_parts = own_rows(residual)

    tile_spec = pl.BlockSpec((1, block_size, block_size), lambda s, *p: (s, 0, 0))
    routed_spec = pl.BlockSpec((plane, 1, half, block_size), lambda s, *p: (0, s, 0, 0))
    whole_spec = pl.BlockSpec((x_count, sample_dev, var_dev), lambda s, *p: (0, 0, 0))
    keep, give = pl.pallas_call(
        functools.partial(product_kernel, x_count),
        out_shape=[shape(x_count, sample_dev, var_dev)] * 2,
        grid_spec=pltpu.PrefetchScalarGridSpec(
            num_scalar_prefetch=3,
            grid=(tile_dev,),
            in_specs=[routed_spec, tile_spec],
            out_specs=[whole_spec, whole_spec],
            scratch_shapes=[pltpu.VMEM((blocks_dev, sample_all, block_size), f32)],
        ),
        name="products",
    )(row_local, is_diag, place, routed_resid, omega_tiles)
    got = swap_core(give)
    arrived = [shift_x(keep[dx] + got[dx], dx) for dx in range(1, x_count)]
    applied, applied_near, applied_far = pl.pallas_call(
        functools.partial(applied_kernel, len(arrived)),
        out_shape=[shape(sample_dev, var_dev), shape(half, var_dev), shape(half, var_dev)],
        grid=(1,),
        in_specs=[
            pl.BlockSpec((1, sample_dev, var_dev), lambda s: (0, 0, 0)),
            pl.BlockSpec((1, sample_dev, var_dev), lambda s: (0, 0, 0)),
            pl.BlockSpec((sample_dev, var_dev), lambda s: (0, 0)),
            pl.BlockSpec((1, var_dev), lambda s: (0, 0)),
        ]
        + [pl.BlockSpec((sample_dev, var_dev), lambda s: (0, 0))] * len(arrived),
        out_specs=[
            pl.BlockSpec((sample_dev, var_dev), lambda s: (0, 0)),
            pl.BlockSpec((half, var_dev), lambda s: (0, 0)),
            pl.BlockSpec((half, var_dev), lambda s: (0, 0)),
        ],
        name="applied",
    )(keep, got, residual, omega_diagonal.reshape(1, var_dev), *arrived)

    routed_applied = route(applied_near, applied_far)
    applied_parts = own_rows(applied)

    diag_spec = pl.BlockSpec((1, var_dev), lambda s, *p: (0, 0))
    new_tiles, new_diagonal = pl.pallas_call(
        functools.partial(gradient_kernel, x_count, 0.5 / sample_all),
        out_shape=[shape(tile_dev, block_size, block_size), shape(1, var_dev)],
        grid_spec=pltpu.PrefetchScalarGridSpec(
            num_scalar_prefetch=3,
            grid=(tile_dev,),
            in_specs=[routed_spec, routed_spec, tile_spec, diag_spec]
            + [any_spec] * (2 * len(resid_parts)),
            out_specs=[tile_spec, diag_spec],
            scratch_shapes=[
                pltpu.VMEM((sample_all, var_dev), f32),
                pltpu.VMEM((sample_all, var_dev), f32),
                pltpu.SemaphoreType.DMA((2, len(resid_parts), 2)),
            ],
        ),
        name="gradients",
    )(
        row_local,
        is_diag,
        place,
        routed_resid,
        routed_applied,
        omega_tiles,
        omega_diagonal.reshape(1, var_dev),
        *resid_parts,
        *applied_parts,
    )
    return new_tiles, new_diagonal.reshape(var_dev)


def solution(mesh):
    rows, cols = mesh.shape["rows"], mesh.shape["cols"]
    fine = Mesh(mesh.devices.reshape(rows // 4, 2, 2, cols // 2, 2), ROWS + COLS)
    placed = (
        P(COLS, ROWS),
        P(None, ROWS),
        P(ROWS + COLS, None, None),
        P(ROWS),
        P(),
        P(),
    )
    return jax.shard_map(
        per_device,
        mesh=fine,
        in_specs=placed,
        out_specs=(P(ROWS + COLS, None, None), P(ROWS)),
        check_vma=False,
    )
```

```python
import functools

import jax
import jax.numpy as jnp
from jax import lax
from jax.experimental import pallas as pl
from jax.experimental.pallas import tpu as pltpu
from jax.sharding import Mesh
from jax.sharding import PartitionSpec as P

step_size = 0.5
penalty = 0.02

ROWS = ("a", "u", "v")
COLS = ("x", "k")
PLANE = ("u", "v", "x")


NT = (((1,), (1,)), ((), ()))
NN = (((1,), (0,)), ((), ()))
TN = (((0,), (0,)), ((), ()))


def dot(left, right, dims):
    return lax.dot_general(left, right, dims, preferred_element_type=jnp.float32)


def split(value, pieces):
    found = []
    for _ in range(pieces):
        piece = value.astype(jnp.bfloat16)
        found.append(piece)
        value = value - piece.astype(jnp.float32)
    return found


def score_kernel(samples, loadings, out):
    rows = samples.shape[0]
    found = dot(jnp.concatenate(split(samples[...], 3), 0), loadings[...], NT)
    value = (found[2 * rows :] + found[rows : 2 * rows]) + found[:rows]
    for copy in range(out.shape[0]):
        out[copy] = value


def residual_kernel(place, scores, samples, loadings, whole, first, second):
    rows, variables = samples.shape
    half = rows // 2
    value = scores[0]
    for source in range(1, scores.shape[0]):
        value = value + scores[source]
    pieces = jnp.concatenate(split(value, 3), 0)
    upper = place[1] == 1
    width = variables // 4
    for at in range(0, variables, width):
        here = slice(at, at + width)
        fitted = dot(pieces, loadings[:, here], NN)
        value = samples[:, here] - ((fitted[2 * rows :] + fitted[rows : 2 * rows]) + fitted[:rows])
        low, high = value[:half], value[half:]
        near = jnp.where(upper, high, low)
        far = jnp.where(upper, low, high)
        whole[:half, here] = near
        whole[half:, here] = far
        first[:, here] = near
        second[:, here] = far


def gather_kernel(count, index, *refs):
    sources = refs[:count]
    out, held, sem, out_sem = refs[-4:]
    copies = [
        pltpu.make_async_copy(source, held.at[at], sem.at[at]) for at, source in enumerate(sources)
    ]
    for copy in copies:
        copy.start()
    for copy in copies:
        copy.wait()
    slots, half, width = out.shape
    blocks = held.shape[2] // width

    def move(slot, carry):
        code = index[slot]
        start = pl.multiple_of((code % blocks) * width, width)
        pltpu.make_async_copy(
            held.at[code // blocks, :, pl.ds(start, width)], out.at[slot], out_sem
        ).start()
        return carry

    lax.fori_loop(0, slots, move, 0, unroll=8)
    pltpu.make_async_copy(out, out, out_sem).wait()


def masked(tile, is_diag):
    size = tile.shape[0]
    row = lax.broadcasted_iota(jnp.int32, (size, size), 0)
    col = lax.broadcasted_iota(jnp.int32, (size, size), 1)
    return jnp.where((row == col) & (is_diag == 1), 0.0, tile)


def tile_kernel(is_diag, tiles, after, high, low):
    high[0], low[0] = split(masked(tiles[0], is_diag[pl.program_id(0)]), 2)


def product_kernel(x_count, row_local, place, routed, tile_hi, tile_lo, keep, give, total):
    step = pl.program_id(0)

    @pl.when(step == 0)
    def _():
        total[...] = jnp.zeros_like(total)

    block = total.shape[2]
    samples = total.shape[1]
    source_hi, source_lo = split(routed[...].reshape(samples, block), 2)
    stacked = dot(jnp.concatenate([source_hi, source_lo], 0), tile_hi[0], NT)
    product = stacked[:samples] + (stacked[samples:] + dot(source_hi, tile_lo[0], NT))
    total[row_local[step]] += product

    @pl.when(step == pl.num_programs(0) - 1)
    def _():
        half = keep.shape[1] // 2
        for out, core in ((keep, place[4]), (give, 1 - place[4])):
            for dx in range(x_count):
                for du in range(2):
                    source = ((place[1] ^ du) * 2 + core) * x_count + (place[3] + dx) % x_count
                    start = pl.multiple_of(source * half, half)
                    for at in range(total.shape[0]):
                        out[dx, du * half : (du + 1) * half, at * block : (at + 1) * block] = total[
                            at, pl.ds(start, half), :
                        ]


def applied_kernel(count, *refs):
    keep, got, residual, diagonal = refs[:4]
    arrived = refs[4 : 4 + count]
    whole, first, second = refs[4 + count :]
    half = first.shape[0]
    value = keep[0] + got[0]
    for other in arrived:
        value = value + other[...]
    value = value + diagonal[...] * residual[...]
    whole[...] = value
    first[...] = value[:half]
    second[...] = value[half:]


def fetch_rows(x_count, place, parts, rows, sem):
    half = parts[0].shape[0] // 2
    copies = []
    for dk in range(2):
        for dx in range(x_count):
            for du in range(2):
                at = dk * x_count + dx
                target = ((place[1] ^ du) * 2 + (place[4] ^ dk)) * x_count + (
                    place[3] + x_count - dx
                ) % x_count
                start = pl.multiple_of(target * half, half)
                copies.append(
                    pltpu.make_async_copy(
                        parts[at].at[du * half : (du + 1) * half],
                        rows.at[pl.ds(start, half)],
                        sem.at[at, du],
                    )
                )
    for copy in copies:
        copy.start()
    for copy in copies:
        copy.wait()


def left_operand(rows):
    high, low = split(rows.T, 2)
    return jnp.concatenate([high, high, low], 1)


def right_operand(rows):
    high, low = split(rows, 2)
    return jnp.concatenate([high, low, high], 0)


def row_kernel(x_count, place, after, *refs):
    parts, (whole, left, rows, sem) = refs[:-4], refs[-4:]
    fetch_rows(x_count, place, parts, rows, sem)
    whole[...] = rows[...]
    block = left.shape[1]
    for at in range(left.shape[0]):
        left[at] = left_operand(rows[:, at * block : (at + 1) * block])


def first_kernel(
    x_count, scale, row_local, place, routed, tiles, diagonal, resid_rows, after, *refs
):
    parts, (partial, new_diagonal, rows, left, sem) = refs[:-5], refs[-5:]
    step = pl.program_id(0)
    block = tiles.shape[2]
    samples = rows.shape[0]

    @pl.when(step == 0)
    def _():
        fetch_rows(x_count, place, parts, rows, sem)
        for at in range(left.shape[0]):
            left[at] = left_operand(rows[:, at * block : (at + 1) * block])
        stat = jnp.sum(rows[...] * resid_rows[...], axis=0, keepdims=True) / samples
        new_diagonal[...] = diagonal[...] - step_size * (stat - 1.0 / diagonal[...])

    right = right_operand(routed[...].reshape(samples, block))
    partial[0] = tiles[0] - step_size * scale * dot(left[row_local[step]], right, NN)


def last_kernel(scale, row_local, is_diag, routed, left, partial, new_tiles):
    block = partial.shape[2]
    right = right_operand(routed[...].reshape(-1, block))
    stepped = partial[0] - step_size * scale * dot(left[0], right, NN)
    stepped = masked(stepped, is_diag[pl.program_id(0)])
    bound = step_size * penalty
    new_tiles[0] = stepped - jnp.clip(stepped, -bound, bound)


def per_device(samples, loadings, omega_tiles, omega_diagonal, tile_rows, tile_cols):
    f32 = jnp.float32
    a_count, x_count = lax.axis_size("a"), lax.axis_size("x")
    row_count, col_count = 4 * a_count, 2 * x_count
    a, u, v, x, k = (lax.axis_index(name) for name in ROWS + COLS)
    my_row = (a * 2 + u) * 2 + v
    sample_dev, var_dev = samples.shape
    half = sample_dev // 2
    sample_all = sample_dev * col_count
    factors = loadings.shape[0]
    tile_dev, block_size = omega_tiles.shape[:2]
    blocks_dev = var_dev // block_size
    plane = 4 * x_count
    any_spec = pl.BlockSpec(memory_space=pl.ANY)
    vmem = pl.BlockSpec(memory_space=pltpu.VMEM)
    small = pltpu.CompilerParams(vmem_limit_bytes=16 * 1024 * 1024)

    def cost(flops, moved):
        return pl.CostEstimate(flops=flops, bytes_accessed=moved, transcendentals=0)

    shape = lambda *dims: jax.ShapeDtypeStruct(dims, f32)

    place = jnp.stack([a, u, v, x, k]).astype(jnp.int32)
    my_tiles = (my_row * col_count + x * 2 + k) * tile_dev
    my_rows = lax.dynamic_slice_in_dim(tile_rows, my_tiles, tile_dev)
    my_cols = lax.dynamic_slice_in_dim(tile_cols, my_tiles, tile_dev)
    row_local = my_rows - my_row * blocks_dev
    is_diag = (my_rows == my_cols).astype(jnp.int32)
    wanted = tile_cols.reshape(a_count, 2, 2, x_count, 2, tile_dev)
    wanted = lax.dynamic_index_in_dim(wanted, a, 0, keepdims=False)
    wanted = lax.dynamic_index_in_dim(wanted, k, 3, keepdims=False).reshape(plane * tile_dev)
    group = wanted // blocks_dev
    slot_index = (
        (((a + a_count - group // 4) % a_count) * 2 + (((group // 2) % 2) ^ u)) * 2
        + ((group % 2) ^ k)
    ) * blocks_dev + wanted % blocks_dev

    def permute(value, names, target):
        sizes = [lax.axis_size(name) for name in names]

        def flat(coords):
            at = 0
            for coord, size in zip(coords, sizes):
                at = at * size + coord
            return at

        def coords_of(at):
            coords = []
            for size in reversed(sizes):
                coords.append(at % size)
                at //= size
            return tuple(reversed(coords))

        total = 1
        for size in sizes:
            total *= size
        return lax.ppermute(
            value, names, [(at, flat(target(*coords_of(at)))) for at in range(total)]
        )

    def swap_core(value):
        return permute(value, ("k",), lambda k: (1 - k,))

    def shift_x(value, dx):
        return permute(value, ("x",), lambda x: ((x + dx) % x_count,))

    smem = pl.BlockSpec(memory_space=pltpu.SMEM)
    score_copies = pl.pallas_call(
        score_kernel,
        out_shape=shape(row_count, sample_dev, factors),
        in_specs=[vmem, vmem],
        out_specs=vmem,
        name="scores",
    )(samples, loadings)
    score_terms = lax.all_to_all(score_copies, ROWS, 0, 0, tiled=True)
    residual, resid_near, resid_far = pl.pallas_call(
        residual_kernel,
        out_shape=[shape(sample_dev, var_dev), shape(half, var_dev), shape(half, var_dev)],
        in_specs=[smem, vmem, vmem, vmem],
        out_specs=[vmem] * 3,
        name="residual",
    )(place, score_terms, samples, loadings)

    def route(near, far, beside):
        held = []
        for da in range(a_count):
            for dz, part in enumerate((near, far)):
                held.append(
                    permute(
                        part,
                        ("a", "u", "v", "k"),
                        lambda a, u, v, k: ((a + da) % a_count, u ^ dz, k, v),
                    )
                )
        sources = []
        for part in held:
            sources += [part, swap_core(part)]
        return pl.pallas_call(
            functools.partial(gather_kernel, len(sources)),
            out_shape=shape(plane * tile_dev, half, block_size),
            in_specs=[smem] + [any_spec] * (len(sources) + len(beside)),
            out_specs=any_spec,
            scratch_shapes=[
                pltpu.VMEM((len(sources), half, var_dev), f32),
                pltpu.SemaphoreType.DMA((len(sources),)),
                pltpu.SemaphoreType.DMA,
            ],
            compiler_params=small,
            name="gather_slots",
        )(slot_index, *sources, *beside)

    def deliver(slots):
        return lax.all_to_all(
            slots.reshape(plane, tile_dev, half, block_size), PLANE, 0, 0, tiled=True
        )

    def own_rows(whole):
        parts = [whole] + [shift_x(whole, dx) for dx in range(1, x_count)]
        return parts + [swap_core(part) for part in parts]

    tile_spec = pl.BlockSpec((1, block_size, block_size), lambda s, *p: (s, 0, 0))
    routed_spec = pl.BlockSpec((plane, 1, half, block_size), lambda s, *p: (0, s, 0, 0))
    whole_spec = pl.BlockSpec((x_count, sample_dev, var_dev), lambda s, *p: (0, 0, 0))
    diag_spec = pl.BlockSpec((1, var_dev), lambda s, *p: (0, 0))
    rows_spec = pl.BlockSpec((sample_all, var_dev), lambda s, *p: (0, 0))
    diagonal = omega_diagonal.reshape(1, var_dev)
    depth = 3 * sample_all
    left_shape = (blocks_dev, block_size, depth)
    tile_elements = tile_dev * block_size * block_size
    scale = 0.5 / sample_all

    resid_parts = own_rows(residual)
    resid_slots = route(resid_near, resid_far, resid_parts)
    routed_resid = deliver(resid_slots)
    tiles_hi, tiles_lo = pl.pallas_call(
        tile_kernel,
        out_shape=[jax.ShapeDtypeStruct(omega_tiles.shape, jnp.bfloat16)] * 2,
        grid_spec=pltpu.PrefetchScalarGridSpec(
            num_scalar_prefetch=1,
            grid=(tile_dev,),
            in_specs=[tile_spec, any_spec],
            out_specs=[tile_spec, tile_spec],
        ),
        cost_estimate=cost(0, 8 * tile_elements),
        name="split_tiles",
    )(is_diag, omega_tiles, resid_slots)
    resid_rows, resid_left = pl.pallas_call(
        functools.partial(row_kernel, x_count),
        out_shape=[
            shape(sample_all, var_dev),
            jax.ShapeDtypeStruct(left_shape, jnp.bfloat16),
        ],
        in_specs=[smem] + [any_spec] * (1 + len(resid_parts)),
        out_specs=[vmem, vmem],
        scratch_shapes=[
            pltpu.VMEM((sample_all, var_dev), f32),
            pltpu.SemaphoreType.DMA((2 * x_count, 2)),
        ],
        cost_estimate=cost(0, 16 * sample_all * var_dev),
        name="resid_rows",
    )(place, resid_slots, *resid_parts)

    keep, give = pl.pallas_call(
        functools.partial(product_kernel, x_count),
        out_shape=[shape(x_count, sample_dev, var_dev)] * 2,
        grid_spec=pltpu.PrefetchScalarGridSpec(
            num_scalar_prefetch=2,
            grid=(tile_dev,),
            in_specs=[routed_spec, tile_spec, tile_spec],
            out_specs=[whole_spec, whole_spec],
            scratch_shapes=[pltpu.VMEM((blocks_dev, sample_all, block_size), f32)],
        ),
        name="products",
    )(row_local, place, routed_resid, tiles_hi, tiles_lo)
    got = swap_core(give)
    arrived = [shift_x(keep[dx] + got[dx], dx) for dx in range(1, x_count)]
    applied, applied_near, applied_far = pl.pallas_call(
        functools.partial(applied_kernel, len(arrived)),
        out_shape=[shape(sample_dev, var_dev), shape(half, var_dev), shape(half, var_dev)],
        grid=(1,),
        in_specs=[
            pl.BlockSpec((1, sample_dev, var_dev), lambda s: (0, 0, 0)),
            pl.BlockSpec((1, sample_dev, var_dev), lambda s: (0, 0, 0)),
            pl.BlockSpec((sample_dev, var_dev), lambda s: (0, 0)),
            pl.BlockSpec((1, var_dev), lambda s: (0, 0)),
        ]
        + [pl.BlockSpec((sample_dev, var_dev), lambda s: (0, 0))] * len(arrived),
        out_specs=[
            pl.BlockSpec((sample_dev, var_dev), lambda s: (0, 0)),
            pl.BlockSpec((half, var_dev), lambda s: (0, 0)),
            pl.BlockSpec((half, var_dev), lambda s: (0, 0)),
        ],
        name="applied",
    )(keep, got, residual, diagonal, *arrived)

    applied_parts = own_rows(applied)
    applied_slots = route(applied_near, applied_far, applied_parts)
    routed_applied = deliver(applied_slots)
    partial, new_diagonal = pl.pallas_call(
        functools.partial(first_kernel, x_count, scale),
        out_shape=[shape(*omega_tiles.shape), shape(1, var_dev)],
        grid_spec=pltpu.PrefetchScalarGridSpec(
            num_scalar_prefetch=2,
            grid=(tile_dev,),
            in_specs=[routed_spec, tile_spec, diag_spec, rows_spec, any_spec]
            + [any_spec] * len(applied_parts),
            out_specs=[tile_spec, diag_spec],
            scratch_shapes=[
                pltpu.VMEM((sample_all, var_dev), f32),
                pltpu.VMEM(left_shape, jnp.bfloat16),
                pltpu.SemaphoreType.DMA((2 * x_count, 2)),
            ],
        ),
        cost_estimate=cost(2 * depth * tile_elements, 16 * tile_elements),
        name="first_term",
    )(
        row_local,
        place,
        routed_resid,
        omega_tiles,
        diagonal,
        resid_rows,
        applied_slots,
        *applied_parts,
    )
    new_tiles = pl.pallas_call(
        functools.partial(last_kernel, scale),
        out_shape=shape(*omega_tiles.shape),
        grid_spec=pltpu.PrefetchScalarGridSpec(
            num_scalar_prefetch=2,
            grid=(tile_dev,),
            in_specs=[
                routed_spec,
                pl.BlockSpec((1, block_size, depth), lambda s, rows, *p: (rows[s], 0, 0)),
                tile_spec,
            ],
            out_specs=tile_spec,
        ),
        name="last_term",
    )(row_local, is_diag, routed_applied, resid_left, partial)
    return new_tiles, new_diagonal.reshape(var_dev)


def solution(mesh):
    rows, cols = mesh.shape["rows"], mesh.shape["cols"]
    fine = Mesh(mesh.devices.reshape(rows // 4, 2, 2, cols // 2, 2), ROWS + COLS)
    placed = (
        P(COLS, ROWS),
        P(None, ROWS),
        P(ROWS + COLS, None, None),
        P(ROWS),
        P(),
        P(),
    )
    return jax.shard_map(
        per_device,
        mesh=fine,
        in_specs=placed,
        out_specs=(P(ROWS + COLS, None, None), P(ROWS)),
        check_vma=False,
    )
```

```python
import functools

import jax
import jax.numpy as jnp
from jax import lax
from jax.experimental import pallas as pl
from jax.experimental.pallas import tpu as pltpu
from jax.sharding import Mesh
from jax.sharding import PartitionSpec as P

step_size = 0.5
penalty = 0.02

ROWS = ("a", "u", "v")
COLS = ("x", "k")
PLANE = ("u", "v", "x")


NT = (((1,), (1,)), ((), ()))
NN = (((1,), (0,)), ((), ()))
TN = (((0,), (0,)), ((), ()))


def dot(left, right, dims):
    return lax.dot_general(left, right, dims, preferred_element_type=jnp.float32)


def split(value, pieces):
    found = []
    for _ in range(pieces):
        piece = value.astype(jnp.bfloat16)
        found.append(piece)
        value = value - piece.astype(jnp.float32)
    return found


def score_kernel(samples, loadings, out, held, sem):
    rows, variables = samples.shape
    chunks = sem.shape[0]
    width = variables // chunks
    copies = [
        pltpu.make_async_copy(
            loadings.at[:, at * width : (at + 1) * width],
            held.at[:, at * width : (at + 1) * width],
            sem.at[at],
        )
        for at in range(chunks)
    ]
    for copy in copies:
        copy.start()
    found = None
    for at, copy in enumerate(copies):
        here = slice(at * width, (at + 1) * width)
        pieces = jnp.concatenate(split(samples[:, here], 3), 0)
        copy.wait()
        term = dot(pieces, held[:, here], NT)
        found = term if found is None else found + term
    value = (found[2 * rows :] + found[rows : 2 * rows]) + found[:rows]
    for copy in range(out.shape[0]):
        out[copy] = value


def residual_kernel(place, scores, samples, loadings, whole, first, second):
    rows, variables = samples.shape
    half = rows // 2
    value = scores[0]
    for source in range(1, scores.shape[0]):
        value = value + scores[source]
    pieces = jnp.concatenate(split(value, 3), 0)
    upper = place[1] == 1
    width = variables // 4
    for at in range(0, variables, width):
        here = slice(at, at + width)
        fitted = dot(pieces, loadings[:, here], NN)
        value = samples[:, here] - ((fitted[2 * rows :] + fitted[rows : 2 * rows]) + fitted[:rows])
        low, high = value[:half], value[half:]
        near = jnp.where(upper, high, low)
        far = jnp.where(upper, low, high)
        whole[:half, here] = near
        whole[half:, here] = far
        first[:, here] = near
        second[:, here] = far


def gather_kernel(count, index, *refs):
    sources = refs[:count]
    out, held = refs[-2:]
    for at, source in enumerate(sources):
        held[at] = source[...]
    slots, half, width = out.shape
    blocks = held.shape[2] // width

    def move(slot, carry):
        code = index[slot]
        start = pl.multiple_of((code % blocks) * width, width)
        out[slot] = held[code // blocks, :, pl.ds(start, width)]
        return carry

    lax.fori_loop(0, slots, move, 0, unroll=8)


def masked(tile, is_diag):
    size = tile.shape[0]
    row = lax.broadcasted_iota(jnp.int32, (size, size), 0)
    col = lax.broadcasted_iota(jnp.int32, (size, size), 1)
    return jnp.where((row == col) & (is_diag == 1), 0.0, tile)


def fetch_tiles(tiles, held, sem):
    copies = [
        pltpu.make_async_copy(tiles.at[at], held.at[at], sem.at[at]) for at in range(tiles.shape[0])
    ]
    for copy in copies:
        copy.start()


def tile_kernel(is_diag, tiles, after, high, low, held, sem):
    fetch_tiles(tiles, held, sem)

    def convert(at, carry):
        pltpu.make_async_copy(tiles.at[at], held.at[at], sem.at[at]).wait()
        high[at], low[at] = split(masked(held[at], is_diag[at]), 2)
        return carry

    lax.fori_loop(0, tiles.shape[0], convert, 0)


def product_kernel(x_count, row_local, place, routed, tile_hi, tile_lo, keep, give, total):
    blocks, samples, block = total.shape
    total[...] = jnp.zeros_like(total)

    def multiply(at, carry):
        source_hi, source_lo = split(routed[:, pl.ds(at, 1)].reshape(samples, block), 2)
        stacked = dot(jnp.concatenate([source_hi, source_lo], 0), tile_hi[at], NT)
        product = stacked[:samples] + (stacked[samples:] + dot(source_hi, tile_lo[at], NT))
        total[row_local[at]] += product
        return carry

    lax.fori_loop(0, tile_hi.shape[0], multiply, 0)
    half = keep.shape[1] // 2
    for out, core in ((keep, place[4]), (give, 1 - place[4])):
        for dx in range(x_count):
            for du in range(2):
                source = ((place[1] ^ du) * 2 + core) * x_count + (place[3] + dx) % x_count
                start = pl.multiple_of(source * half, half)
                for at in range(blocks):
                    out[dx, du * half : (du + 1) * half, at * block : (at + 1) * block] = total[
                        at, pl.ds(start, half), :
                    ]


def applied_kernel(count, *refs):
    keep, got, residual, diagonal = refs[:4]
    arrived = refs[4 : 4 + count]
    whole, first, second = refs[4 + count :]
    half = first.shape[0]
    value = keep[0] + got[0]
    for other in arrived:
        value = value + other[...]
    value = value + diagonal[...] * residual[...]
    whole[...] = value
    first[...] = value[:half]
    second[...] = value[half:]


def place_rows(x_count, place, parts, rows):
    half = parts[0].shape[0] // 2
    for dk in range(2):
        for dx in range(x_count):
            for du in range(2):
                target = ((place[1] ^ du) * 2 + (place[4] ^ dk)) * x_count + (
                    place[3] + x_count - dx
                ) % x_count
                start = pl.multiple_of(target * half, half)
                rows[pl.ds(start, half)] = parts[dk * x_count + dx][du * half : (du + 1) * half]


def left_operand(rows):
    high, low = split(rows.T, 2)
    return jnp.concatenate([high, high, low], 1)


def right_operand(rows):
    high, low = split(rows, 2)
    return jnp.concatenate([high, low, high], 0)


def row_kernel(x_count, place, after, *refs):
    parts, (rows, left) = refs[:-2], refs[-2:]
    place_rows(x_count, place, parts, rows)
    block = left.shape[1]
    for at in range(left.shape[0]):
        left[at] = left_operand(rows[:, at * block : (at + 1) * block])


def first_kernel(
    x_count, scale, row_local, place, routed, tiles, diagonal, resid_rows, after, *refs
):
    parts, (partial, new_diagonal, rows, left, sem) = refs[:-5], refs[-5:]
    fetch_tiles(tiles, partial, sem)
    samples = rows.shape[0]
    block = left.shape[1]
    place_rows(x_count, place, parts, rows)
    for at in range(left.shape[0]):
        left[at] = left_operand(rows[:, at * block : (at + 1) * block])
    stat = jnp.sum(rows[...] * resid_rows[...], axis=0, keepdims=True) / samples
    new_diagonal[...] = diagonal[...] - step_size * (stat - 1.0 / diagonal[...])

    def subtract(at, carry):
        right = right_operand(routed[:, pl.ds(at, 1)].reshape(samples, block))
        term = dot(left[row_local[at]], right, NN)
        pltpu.make_async_copy(tiles.at[at], partial.at[at], sem.at[at]).wait()
        partial[at] = partial[at] - step_size * scale * term
        return carry

    lax.fori_loop(0, tiles.shape[0], subtract, 0)


def last_kernel(scale, row_local, is_diag, routed, left, partial, new_tiles, held, sem):
    block = partial.shape[2]
    bound = step_size * penalty

    def finish(at, carry):
        right = right_operand(routed[:, pl.ds(at, 1)].reshape(-1, block))
        stepped = partial[at] - step_size * scale * dot(left[row_local[at]], right, NN)
        stepped = masked(stepped, is_diag[at])
        held[at] = stepped - jnp.clip(stepped, -bound, bound)
        pltpu.make_async_copy(held.at[at], new_tiles.at[at], sem.at[at]).start()
        return carry

    lax.fori_loop(0, partial.shape[0], finish, 0)
    for at in range(partial.shape[0]):
        pltpu.make_async_copy(held.at[at], new_tiles.at[at], sem.at[at]).wait()


def per_device(samples, loadings, omega_tiles, omega_diagonal, tile_rows, tile_cols):
    f32 = jnp.float32
    a_count, x_count = lax.axis_size("a"), lax.axis_size("x")
    row_count, col_count = 4 * a_count, 2 * x_count
    a, u, v, x, k = (lax.axis_index(name) for name in ROWS + COLS)
    my_row = (a * 2 + u) * 2 + v
    sample_dev, var_dev = samples.shape
    half = sample_dev // 2
    sample_all = sample_dev * col_count
    factors = loadings.shape[0]
    tile_dev, block_size = omega_tiles.shape[:2]
    blocks_dev = var_dev // block_size
    plane = 4 * x_count
    any_spec = pl.BlockSpec(memory_space=pl.ANY)
    vmem = pl.BlockSpec(memory_space=pltpu.VMEM)
    def cost(flops, moved):
        return pl.CostEstimate(flops=flops, bytes_accessed=moved, transcendentals=0)

    shape = lambda *dims: jax.ShapeDtypeStruct(dims, f32)

    place = jnp.stack([a, u, v, x, k]).astype(jnp.int32)
    my_tiles = (my_row * col_count + x * 2 + k) * tile_dev
    my_rows = lax.dynamic_slice_in_dim(tile_rows, my_tiles, tile_dev)
    my_cols = lax.dynamic_slice_in_dim(tile_cols, my_tiles, tile_dev)
    row_local = my_rows - my_row * blocks_dev
    is_diag = (my_rows == my_cols).astype(jnp.int32)
    wanted = tile_cols.reshape(a_count, 2, 2, x_count, 2, tile_dev)
    wanted = lax.dynamic_index_in_dim(wanted, a, 0, keepdims=False)
    wanted = lax.dynamic_index_in_dim(wanted, k, 3, keepdims=False).reshape(plane * tile_dev)
    group = wanted // blocks_dev
    slot_index = (
        (((a + a_count - group // 4) % a_count) * 2 + (((group // 2) % 2) ^ u)) * 2
        + ((group % 2) ^ k)
    ) * blocks_dev + wanted % blocks_dev

    def permute(value, names, target):
        sizes = [lax.axis_size(name) for name in names]

        def flat(coords):
            at = 0
            for coord, size in zip(coords, sizes):
                at = at * size + coord
            return at

        def coords_of(at):
            coords = []
            for size in reversed(sizes):
                coords.append(at % size)
                at //= size
            return tuple(reversed(coords))

        total = 1
        for size in sizes:
            total *= size
        return lax.ppermute(
            value, names, [(at, flat(target(*coords_of(at)))) for at in range(total)]
        )

    def swap_core(value):
        return permute(value, ("k",), lambda k: (1 - k,))

    def shift_x(value, dx):
        return permute(value, ("x",), lambda x: ((x + dx) % x_count,))

    def call(kernel, name, outs, operands, scratch=(), limit=24, estimate=None):
        arrays, specs = [], []
        for array, spec in operands:
            if spec is vmem:
                array = pltpu.with_memory_space_constraint(array, pltpu.VMEM)
            arrays.append(array)
            specs.append(spec)
        return pl.pallas_call(
            kernel,
            out_shape=[out for out, _ in outs],
            in_specs=specs,
            out_specs=[spec for _, spec in outs],
            scratch_shapes=list(scratch),
            compiler_params=pltpu.CompilerParams(vmem_limit_bytes=limit * 1024 * 1024),
            cost_estimate=estimate,
            name=name,
        )(*arrays)

    def chip(dims, dtype=f32):
        return (pltpu.VMEM(dims, dtype), vmem)

    smem = pl.BlockSpec(memory_space=pltpu.SMEM)
    bf16 = jnp.bfloat16
    diagonal = omega_diagonal.reshape(1, var_dev)
    depth = 3 * sample_all
    tile_elements = tile_dev * block_size * block_size
    tile_sem = pltpu.SemaphoreType.DMA((tile_dev,))
    tile_shape = omega_tiles.shape
    scale = 0.5 / sample_all
    field_outs = [chip((sample_dev, var_dev)), chip((half, var_dev)), chip((half, var_dev))]

    score_copies, held_loadings = call(
        score_kernel,
        "scores",
        [chip((row_count, sample_dev, factors)), chip(loadings.shape, bf16)],
        [(samples, vmem), (loadings, any_spec)],
        [pltpu.SemaphoreType.DMA((4,))],
    )
    score_terms = lax.all_to_all(score_copies, ROWS, 0, 0, tiled=True)
    residual, resid_near, resid_far = call(
        residual_kernel,
        "residual",
        field_outs,
        [(place, smem), (score_terms, vmem), (samples, vmem), (held_loadings, vmem)],
    )

    def route(near, far, beside):
        held = []
        for da in range(a_count):
            for dz, part in enumerate((near, far)):
                held.append(
                    permute(
                        part,
                        ("a", "u", "v", "k"),
                        lambda a, u, v, k: ((a + da) % a_count, u ^ dz, k, v),
                    )
                )
        sources = []
        for part in held:
            sources += [part, swap_core(part)]
        return call(
            functools.partial(gather_kernel, len(sources)),
            "gather_slots",
            [chip((plane * tile_dev, half, block_size))],
            [(slot_index, smem)] + [(part, vmem) for part in sources + beside],
            [pltpu.VMEM((len(sources), half, var_dev), f32)],
        )[0]

    def deliver(slots):
        return lax.all_to_all(
            slots.reshape(plane, tile_dev, half, block_size), PLANE, 0, 0, tiled=True
        )

    def own_rows(whole):
        parts = [whole] + [shift_x(whole, dx) for dx in range(1, x_count)]
        return parts + [swap_core(part) for part in parts]

    resid_parts = own_rows(residual)
    resid_slots = route(resid_near, resid_far, resid_parts)
    routed_resid = deliver(resid_slots)
    tiles_hi, tiles_lo = call(
        tile_kernel,
        "split_tiles",
        [chip(tile_shape, bf16), chip(tile_shape, bf16)],
        [(is_diag, smem), (omega_tiles, any_spec), (resid_slots, vmem)],
        [pltpu.VMEM(tile_shape, f32), tile_sem],
        estimate=cost(0, 8 * tile_elements),
    )
    resid_rows, resid_left = call(
        functools.partial(row_kernel, x_count),
        "resid_rows",
        [chip((sample_all, var_dev)), chip((blocks_dev, block_size, depth), bf16)],
        [(place, smem), (resid_slots, vmem)] + [(part, vmem) for part in resid_parts],
        estimate=cost(0, 16 * sample_all * var_dev),
    )

    keep, give = call(
        functools.partial(product_kernel, x_count),
        "products",
        [chip((x_count, sample_dev, var_dev))] * 2,
        [
            (row_local, smem),
            (place, smem),
            (routed_resid, vmem),
            (tiles_hi, vmem),
            (tiles_lo, vmem),
        ],
        [pltpu.VMEM((blocks_dev, sample_all, block_size), f32)],
    )
    got = swap_core(give)
    arrived = [shift_x(keep[dx] + got[dx], dx) for dx in range(1, x_count)]
    applied, applied_near, applied_far = call(
        functools.partial(applied_kernel, len(arrived)),
        "applied",
        field_outs,
        [(part, vmem) for part in (keep, got, residual, diagonal, *arrived)],
    )

    applied_parts = own_rows(applied)
    applied_slots = route(applied_near, applied_far, applied_parts)
    routed_applied = deliver(applied_slots)
    partial, new_diagonal = call(
        functools.partial(first_kernel, x_count, scale),
        "first_term",
        [chip(tile_shape), (shape(1, var_dev), vmem)],
        [
            (row_local, smem),
            (place, smem),
            (routed_resid, vmem),
            (omega_tiles, any_spec),
            (diagonal, vmem),
            (resid_rows, vmem),
            (applied_slots, vmem),
        ]
        + [(part, vmem) for part in applied_parts],
        [
            pltpu.VMEM((sample_all, var_dev), f32),
            pltpu.VMEM((blocks_dev, block_size, depth), bf16),
            tile_sem,
        ],
        estimate=cost(2 * depth * tile_elements, 16 * tile_elements),
    )
    (new_tiles,) = call(
        functools.partial(last_kernel, scale),
        "last_term",
        [(shape(*tile_shape), any_spec)],
        [
            (row_local, smem),
            (is_diag, smem),
            (routed_applied, vmem),
            (resid_left, vmem),
            (partial, vmem),
        ],
        [pltpu.VMEM(tile_shape, f32), tile_sem],
    )
    return new_tiles, new_diagonal.reshape(var_dev)


def solution(mesh):
    rows, cols = mesh.shape["rows"], mesh.shape["cols"]
    fine = Mesh(mesh.devices.reshape(rows // 4, 2, 2, cols // 2, 2), ROWS + COLS)
    placed = (
        P(COLS, ROWS),
        P(None, ROWS),
        P(ROWS + COLS, None, None),
        P(ROWS),
        P(),
        P(),
    )
    return jax.shard_map(
        per_device,
        mesh=fine,
        in_specs=placed,
        out_specs=(P(ROWS + COLS, None, None), P(ROWS)),
        check_vma=False,
    )
```

```python
import functools

import jax
import jax.numpy as jnp
from jax import lax
from jax.experimental import pallas as pl
from jax.experimental.pallas import tpu as pltpu
from jax.sharding import Mesh
from jax.sharding import PartitionSpec as P

step_size = 0.5
penalty = 0.02

ROWS = ("a", "u", "v")
COLS = ("x", "k")
PLANE = ("u", "v", "x")


NT = (((1,), (1,)), ((), ()))
NN = (((1,), (0,)), ((), ()))
TN = (((0,), (0,)), ((), ()))


def dot(left, right, dims):
    return lax.dot_general(left, right, dims, preferred_element_type=jnp.float32)


def split(value, pieces):
    found = []
    for _ in range(pieces):
        piece = value.astype(jnp.bfloat16)
        found.append(piece)
        value = value - piece.astype(jnp.float32)
    return found


def table_kernel(sizes, place, tile_rows, tile_cols, row_local, is_diag, slot_index):
    x_count, blocks = sizes
    a, u, v, x, k = (place[at] for at in range(5))
    tile_dev = row_local.shape[0]

    def first_tile(u, v, x):
        return ((((a * 2 + u) * 2 + v) * x_count + x) * 2 + k) * tile_dev

    mine = first_tile(u, v, x)
    for at in range(tile_dev):
        row, col = tile_rows[mine + at], tile_cols[mine + at]
        row_local[at] = row - ((a * 2 + u) * 2 + v) * blocks
        is_diag[at] = jnp.where(row == col, 1, 0)
    a_count = tile_cols.shape[0] // (8 * x_count * tile_dev)
    peer = 0
    for du in range(2):
        for dv in range(2):
            for dx in range(x_count):
                theirs = first_tile(u ^ du, v ^ dv, lax.rem(x + dx, x_count))
                for at in range(tile_dev):
                    col = tile_cols[theirs + at]
                    group = col // blocks
                    da = lax.rem(a + a_count - group // 4, a_count)
                    part = (da * 2 + (((group // 2) % 2) ^ u)) * 2 + ((group % 2) ^ k)
                    slot_index[peer * tile_dev + at] = part * blocks + col % blocks
                peer += 1


def score_kernel(samples, loadings, out, held_samples, held, sem):
    rows, variables = samples.shape
    chunks = sem.shape[0] - 1
    width = variables // chunks
    whole = pltpu.make_async_copy(samples, held_samples, sem.at[chunks])
    whole.start()
    copies = [
        pltpu.make_async_copy(
            loadings.at[:, at * width : (at + 1) * width],
            held.at[:, at * width : (at + 1) * width],
            sem.at[at],
        )
        for at in range(chunks)
    ]
    for copy in copies:
        copy.start()
    whole.wait()
    found = None
    for at, copy in enumerate(copies):
        here = slice(at * width, (at + 1) * width)
        pieces = jnp.concatenate(split(held_samples[:, here], 3), 0)
        copy.wait()
        term = dot(pieces, held[:, here], NT)
        found = term if found is None else found + term
    value = (found[2 * rows :] + found[rows : 2 * rows]) + found[:rows]
    for copy in range(out.shape[0]):
        out[copy] = value


def residual_kernel(place, scores, samples, loadings, whole, first, second):
    rows, variables = samples.shape
    half = rows // 2
    value = scores[0]
    for source in range(1, scores.shape[0]):
        value = value + scores[source]
    pieces = jnp.concatenate(split(value, 3), 0)
    upper = place[1] == 1
    width = variables // 4
    for at in range(0, variables, width):
        here = slice(at, at + width)
        fitted = dot(pieces, loadings[:, here], NN)
        value = samples[:, here] - ((fitted[2 * rows :] + fitted[rows : 2 * rows]) + fitted[:rows])
        low, high = value[:half], value[half:]
        near = jnp.where(upper, high, low)
        far = jnp.where(upper, low, high)
        whole[:half, here] = near
        whole[half:, here] = far
        first[:, here] = near
        second[:, here] = far


def gather_kernel(count, peers, index, *refs):
    sources, outs, held = refs[:count], refs[-1 - peers : -1], refs[-1]
    for at, source in enumerate(sources):
        held[at] = source[...]
    tile_dev, _, width = outs[0].shape
    blocks = held.shape[2] // width
    for peer, out in enumerate(outs):
        for at in range(tile_dev):
            code = index[peer * tile_dev + at]
            start = pl.multiple_of((code % blocks) * width, width)
            out[at] = held[code // blocks, :, pl.ds(start, width)]


def block_of(routed, at):
    return jnp.concatenate([part[at] for part in routed], 0)


def masked(tile, is_diag):
    size = tile.shape[0]
    row = lax.broadcasted_iota(jnp.int32, (size, size), 0)
    col = lax.broadcasted_iota(jnp.int32, (size, size), 1)
    return jnp.where((row == col) & (is_diag == 1), 0.0, tile)


def fetch_tiles(tiles, held, sem):
    copies = [
        pltpu.make_async_copy(tiles.at[at], held.at[at], sem.at[at]) for at in range(tiles.shape[0])
    ]
    for copy in copies:
        copy.start()


def tile_kernel(is_diag, tiles, after, high, low, held, sem):
    fetch_tiles(tiles, held, sem)

    def convert(at, carry):
        pltpu.make_async_copy(tiles.at[at], held.at[at], sem.at[at]).wait()
        high[at], low[at] = split(masked(held[at], is_diag[at]), 2)
        return carry

    lax.fori_loop(0, tiles.shape[0], convert, 0)


def product_kernel(x_count, row_local, place, tile_hi, tile_lo, *refs):
    routed, (keep, give, total) = refs[:-3], refs[-3:]
    blocks, samples, block = total.shape
    total[...] = jnp.zeros_like(total)

    def multiply(at, carry):
        source_hi, source_lo = split(block_of(routed, at), 2)
        stacked = dot(jnp.concatenate([source_hi, source_lo], 0), tile_hi[at], NT)
        product = stacked[:samples] + (stacked[samples:] + dot(source_hi, tile_lo[at], NT))
        total[row_local[at]] += product
        return carry

    lax.fori_loop(0, tile_hi.shape[0], multiply, 0)
    half = keep.shape[1] // 2
    for out, core in ((keep, place[4]), (give, 1 - place[4])):
        for dx in range(x_count):
            for du in range(2):
                source = (du * 2 + (place[2] ^ core)) * x_count + (x_count - dx) % x_count
                start = pl.multiple_of(source * half, half)
                for at in range(blocks):
                    out[dx, du * half : (du + 1) * half, at * block : (at + 1) * block] = total[
                        at, pl.ds(start, half), :
                    ]


def applied_kernel(count, *refs):
    keep, got, residual, diagonal = refs[:4]
    arrived = refs[4 : 4 + count]
    whole, first, second = refs[4 + count :]
    half = first.shape[0]
    value = keep[0] + got[0]
    for other in arrived:
        value = value + other[...]
    value = value + diagonal[...] * residual[...]
    whole[...] = value
    first[...] = value[:half]
    second[...] = value[half:]


def place_rows(x_count, place, parts, rows):
    half = parts[0].shape[0] // 2
    for dk in range(2):
        for dx in range(x_count):
            for du in range(2):
                target = (du * 2 + (place[2] ^ place[4] ^ dk)) * x_count + dx
                start = pl.multiple_of(target * half, half)
                rows[pl.ds(start, half)] = parts[dk * x_count + dx][du * half : (du + 1) * half]


def left_operand(rows):
    high, low = split(rows.T, 2)
    return jnp.concatenate([high, high, low], 1)


def right_operand(rows):
    high, low = split(rows, 2)
    return jnp.concatenate([high, low, high], 0)


def row_kernel(x_count, place, after, *refs):
    parts, (rows, left) = refs[:-2], refs[-2:]
    place_rows(x_count, place, parts, rows)
    block = left.shape[1]
    for at in range(left.shape[0]):
        left[at] = left_operand(rows[:, at * block : (at + 1) * block])


def first_kernel(x_count, scale, row_local, place, tiles, diagonal, resid_rows, after, *refs):
    inputs, (partial, new_diagonal, rows, left, sem) = refs[:-5], refs[-5:]
    parts, routed = inputs[: 2 * x_count], inputs[2 * x_count :]
    fetch_tiles(tiles, partial, sem)
    samples = rows.shape[0]
    block = left.shape[1]
    place_rows(x_count, place, parts, rows)
    for at in range(left.shape[0]):
        left[at] = left_operand(rows[:, at * block : (at + 1) * block])
    stat = jnp.sum(rows[...] * resid_rows[...], axis=0, keepdims=True) / samples
    new_diagonal[...] = diagonal[...] - step_size * (stat - 1.0 / diagonal[...])

    def subtract(at, carry):
        right = right_operand(block_of(routed, at))
        term = dot(left[row_local[at]], right, NN)
        pltpu.make_async_copy(tiles.at[at], partial.at[at], sem.at[at]).wait()
        partial[at] = partial[at] - step_size * scale * term
        return carry

    lax.fori_loop(0, tiles.shape[0], subtract, 0)


def last_kernel(scale, row_local, is_diag, left, partial, *refs):
    routed, (new_tiles, held, sem) = refs[:-3], refs[-3:]
    bound = step_size * penalty

    def finish(at, carry):
        right = right_operand(block_of(routed, at))
        stepped = partial[at] - step_size * scale * dot(left[row_local[at]], right, NN)
        stepped = masked(stepped, is_diag[at])
        held[at] = stepped - jnp.clip(stepped, -bound, bound)
        pltpu.make_async_copy(held.at[at], new_tiles.at[at], sem.at[at]).start()
        return carry

    lax.fori_loop(0, partial.shape[0], finish, 0)
    for at in range(partial.shape[0]):
        pltpu.make_async_copy(held.at[at], new_tiles.at[at], sem.at[at]).wait()


def per_device(samples, loadings, omega_tiles, omega_diagonal, tile_rows, tile_cols):
    f32 = jnp.float32
    a_count, x_count = lax.axis_size("a"), lax.axis_size("x")
    row_count, col_count = 4 * a_count, 2 * x_count
    a, u, v, x, k = (lax.axis_index(name) for name in ROWS + COLS)
    sample_dev, var_dev = samples.shape
    half = sample_dev // 2
    sample_all = sample_dev * col_count
    factors = loadings.shape[0]
    tile_dev, block_size = omega_tiles.shape[:2]
    blocks_dev = var_dev // block_size
    plane = 4 * x_count
    hbm = pl.BlockSpec(memory_space=pltpu.HBM)
    vmem = pl.BlockSpec(memory_space=pltpu.VMEM)
    def cost(flops, moved):
        return pl.CostEstimate(flops=flops, bytes_accessed=moved, transcendentals=0)

    shape = lambda *dims: jax.ShapeDtypeStruct(dims, f32)

    place = jnp.stack([a, u, v, x, k]).astype(jnp.int32)
    def permute(value, names, target):
        sizes = [lax.axis_size(name) for name in names]

        def flat(coords):
            at = 0
            for coord, size in zip(coords, sizes):
                at = at * size + coord
            return at

        def coords_of(at):
            coords = []
            for size in reversed(sizes):
                coords.append(at % size)
                at //= size
            return tuple(reversed(coords))

        total = 1
        for size in sizes:
            total *= size
        return lax.ppermute(
            value, names, [(at, flat(target(*coords_of(at)))) for at in range(total)]
        )

    def swap_core(value):
        return permute(value, ("k",), lambda k: (1 - k,))

    def shift_x(value, dx):
        return permute(value, ("x",), lambda x: ((x + dx) % x_count,))

    def call(kernel, name, outs, operands, scratch=(), limit=24, estimate=None):
        arrays, specs = [], []
        for array, spec in operands:
            if spec is vmem:
                array = pltpu.with_memory_space_constraint(array, pltpu.VMEM)
            if spec is hbm:
                array = pltpu.with_memory_space_constraint(array, pltpu.HBM)
            arrays.append(array)
            specs.append(spec)
        return pl.pallas_call(
            kernel,
            out_shape=[out for out, _ in outs],
            in_specs=specs,
            out_specs=[spec for _, spec in outs],
            scratch_shapes=list(scratch),
            compiler_params=pltpu.CompilerParams(vmem_limit_bytes=limit * 1024 * 1024),
            cost_estimate=estimate,
            name=name,
        )(*arrays)

    def chip(dims, dtype=f32):
        return (pltpu.VMEM(dims, dtype), vmem)

    smem = pl.BlockSpec(memory_space=pltpu.SMEM)
    bf16 = jnp.bfloat16
    diagonal = omega_diagonal.reshape(1, var_dev)
    depth = 3 * sample_all
    tile_elements = tile_dev * block_size * block_size
    tile_sem = pltpu.SemaphoreType.DMA((tile_dev,))
    tile_shape = omega_tiles.shape
    scale = 0.5 / sample_all
    field_outs = [chip((sample_dev, var_dev)), chip((half, var_dev)), chip((half, var_dev))]

    row_local, is_diag, slot_index = call(
        functools.partial(table_kernel, (x_count, blocks_dev)),
        "tables",
        [
            (jax.ShapeDtypeStruct((count,), jnp.int32), smem)
            for count in (tile_dev, tile_dev, plane * tile_dev)
        ],
        [(place, smem), (tile_rows, smem), (tile_cols, smem)],
    )

    score_copies, held_samples, held_loadings = call(
        score_kernel,
        "scores",
        [
            chip((row_count, sample_dev, factors)),
            chip(samples.shape),
            chip(loadings.shape, bf16),
        ],
        [(samples, hbm), (loadings, hbm)],
        [pltpu.SemaphoreType.DMA((5,))],
    )
    score_terms = lax.all_to_all(score_copies, ROWS, 0, 0, tiled=True)
    residual, resid_near, resid_far = call(
        residual_kernel,
        "residual",
        field_outs,
        [(place, smem), (score_terms, vmem), (held_samples, vmem), (held_loadings, vmem)],
    )

    def route(near, far, beside):
        held = []
        for da in range(a_count):
            for dz, part in enumerate((near, far)):
                held.append(
                    permute(
                        part,
                        ("a", "u", "v", "k"),
                        lambda a, u, v, k: ((a + da) % a_count, u ^ dz, k, v),
                    )
                )
        sources = []
        for part in held:
            sources += [part, swap_core(part)]
        return call(
            functools.partial(gather_kernel, len(sources), plane),
            "gather_slots",
            [chip((tile_dev, half, block_size))] * plane,
            [(slot_index, smem)] + [(part, vmem) for part in sources + beside],
            [pltpu.VMEM((len(sources), half, var_dev), f32)],
        )

    def deliver(slots):
        routed = []
        for at, slot in enumerate(slots):
            du, dv, dx = at // (2 * x_count), (at // x_count) % 2, at % x_count
            if at > 0:
                slot = permute(
                    slot, PLANE, lambda u, v, x: (u ^ du, v ^ dv, (x + dx) % x_count)
                )
            routed.append(slot)
        return routed

    def own_rows(whole):
        parts = [whole] + [shift_x(whole, dx) for dx in range(1, x_count)]
        return parts + [swap_core(part) for part in parts]

    resid_parts = own_rows(residual)
    resid_slots = route(resid_near, resid_far, resid_parts)
    routed_resid = deliver(resid_slots)
    tiles_hi, tiles_lo = call(
        tile_kernel,
        "split_tiles",
        [chip(tile_shape, bf16), chip(tile_shape, bf16)],
        [(is_diag, smem), (omega_tiles, hbm), (resid_slots[0], vmem)],
        [pltpu.VMEM(tile_shape, f32), tile_sem],
        estimate=cost(0, 8 * tile_elements),
    )
    resid_rows, resid_left = call(
        functools.partial(row_kernel, x_count),
        "resid_rows",
        [chip((sample_all, var_dev)), chip((blocks_dev, block_size, depth), bf16)],
        [(place, smem), (resid_slots[0], vmem)] + [(part, vmem) for part in resid_parts],
        estimate=cost(0, 16 * sample_all * var_dev),
    )

    keep, give = call(
        functools.partial(product_kernel, x_count),
        "products",
        [chip((x_count, sample_dev, var_dev))] * 2,
        [
            (row_local, smem),
            (place, smem),
            (tiles_hi, vmem),
            (tiles_lo, vmem),
        ]
        + [(part, vmem) for part in routed_resid],
        [pltpu.VMEM((blocks_dev, sample_all, block_size), f32)],
    )
    got = swap_core(give)
    arrived = [shift_x(keep[dx] + got[dx], dx) for dx in range(1, x_count)]
    applied, applied_near, applied_far = call(
        functools.partial(applied_kernel, len(arrived)),
        "applied",
        field_outs,
        [(part, vmem) for part in (keep, got, residual, diagonal, *arrived)],
    )

    applied_parts = own_rows(applied)
    applied_slots = route(applied_near, applied_far, applied_parts)
    routed_applied = deliver(applied_slots)
    partial, new_diagonal = call(
        functools.partial(first_kernel, x_count, scale),
        "first_term",
        [chip(tile_shape), (shape(1, var_dev), vmem)],
        [
            (row_local, smem),
            (place, smem),
            (omega_tiles, hbm),
            (diagonal, vmem),
            (resid_rows, vmem),
            (applied_slots[0], vmem),
        ]
        + [(part, vmem) for part in applied_parts + routed_resid],
        [
            pltpu.VMEM((sample_all, var_dev), f32),
            pltpu.VMEM((blocks_dev, block_size, depth), bf16),
            tile_sem,
        ],
        estimate=cost(2 * depth * tile_elements, 16 * tile_elements),
    )
    (new_tiles,) = call(
        functools.partial(last_kernel, scale),
        "last_term",
        [(shape(*tile_shape), hbm)],
        [
            (row_local, smem),
            (is_diag, smem),
            (resid_left, vmem),
            (partial, vmem),
        ]
        + [(part, vmem) for part in routed_applied],
        [pltpu.VMEM(tile_shape, f32), tile_sem],
    )
    return new_tiles, new_diagonal.reshape(var_dev)


def solution(mesh):
    rows, cols = mesh.shape["rows"], mesh.shape["cols"]
    fine = Mesh(mesh.devices.reshape(rows // 4, 2, 2, cols // 2, 2), ROWS + COLS)
    placed = (
        P(COLS, ROWS),
        P(None, ROWS),
        P(ROWS + COLS, None, None),
        P(ROWS),
        P(),
        P(),
    )
    return jax.shard_map(
        per_device,
        mesh=fine,
        in_specs=placed,
        out_specs=(P(ROWS + COLS, None, None), P(ROWS)),
        check_vma=False,
    )
```

```python
import functools

import jax
import jax.numpy as jnp
from jax import lax
from jax.experimental import pallas as pl
from jax.experimental.pallas import tpu as pltpu
from jax.sharding import Mesh
from jax.sharding import PartitionSpec as P

step_size = 0.5
penalty = 0.02

ROWS = ("a", "u", "v")
COLS = ("x", "k")
PLANE = ("u", "v", "x")


NT = (((1,), (1,)), ((), ()))
NN = (((1,), (0,)), ((), ()))
TN = (((0,), (0,)), ((), ()))


def dot(left, right, dims):
    return lax.dot_general(left, right, dims, preferred_element_type=jnp.float32)


def split(value, pieces):
    found = []
    for _ in range(pieces):
        piece = value.astype(jnp.bfloat16)
        found.append(piece)
        value = value - piece.astype(jnp.float32)
    return found


def table_kernel(sizes, place, tile_rows, tile_cols, after, row_local, is_diag, slot_index):
    x_count, blocks = sizes
    a, u, v, x, k = (place[at] for at in range(5))
    tile_dev = row_local.shape[0]

    def first_tile(u, v, x):
        return ((((a * 2 + u) * 2 + v) * x_count + x) * 2 + k) * tile_dev

    mine = first_tile(u, v, x)
    for at in range(tile_dev):
        row, col = tile_rows[mine + at], tile_cols[mine + at]
        row_local[at] = row - ((a * 2 + u) * 2 + v) * blocks
        is_diag[at] = jnp.where(row == col, 1, 0)
    a_count = tile_cols.shape[0] // (8 * x_count * tile_dev)
    peer = 0
    for du in range(2):
        for dv in range(2):
            for dx in range(x_count):
                theirs = first_tile(u ^ du, v ^ dv, lax.rem(x + dx, x_count))
                for at in range(tile_dev):
                    col = tile_cols[theirs + at]
                    group = col // blocks
                    da = lax.rem(a + a_count - group // 4, a_count)
                    part = (da * 2 + (((group // 2) % 2) ^ u)) * 2 + ((group % 2) ^ k)
                    slot_index[peer * tile_dev + at] = part * blocks + col % blocks
                peer += 1


def score_kernel(samples, loadings, out, held_samples, held, sem):
    rows, variables = samples.shape
    chunks = sem.shape[0] - 1
    width = variables // chunks
    whole = pltpu.make_async_copy(samples, held_samples, sem.at[chunks])
    whole.start()
    copies = [
        pltpu.make_async_copy(
            loadings.at[:, at * width : (at + 1) * width],
            held.at[:, at * width : (at + 1) * width],
            sem.at[at],
        )
        for at in range(chunks)
    ]
    for copy in copies:
        copy.start()
    whole.wait()
    found = None
    for at, copy in enumerate(copies):
        here = slice(at * width, (at + 1) * width)
        pieces = jnp.concatenate(split(held_samples[:, here], 3), 0)
        copy.wait()
        term = dot(pieces, held[:, here], NT)
        found = term if found is None else found + term
    value = (found[2 * rows :] + found[rows : 2 * rows]) + found[:rows]
    for copy in range(out.shape[0]):
        out[copy] = value


def residual_kernel(place, scores, samples, loadings, after, whole, first, second):
    rows, variables = samples.shape
    half = rows // 2
    value = scores[0]
    for source in range(1, scores.shape[0]):
        value = value + scores[source]
    pieces = jnp.concatenate(split(value, 3), 0)
    upper = place[1] == 1
    width = variables // 4
    for at in range(0, variables, width):
        here = slice(at, at + width)
        fitted = dot(pieces, loadings[:, here], NN)
        value = samples[:, here] - ((fitted[2 * rows :] + fitted[rows : 2 * rows]) + fitted[:rows])
        low, high = value[:half], value[half:]
        near = jnp.where(upper, high, low)
        far = jnp.where(upper, low, high)
        whole[:half, here] = near
        whole[half:, here] = far
        first[:, here] = near
        second[:, here] = far


def gather_kernel(count, peers, index, *refs):
    sources, outs, held = refs[:count], refs[-1 - peers : -1], refs[-1]
    for at, source in enumerate(sources):
        held[at] = source[...]
    tile_dev, _, width = outs[0].shape
    blocks = held.shape[2] // width
    for peer, out in enumerate(outs):
        for at in range(tile_dev):
            code = index[peer * tile_dev + at]
            start = pl.multiple_of((code % blocks) * width, width)
            out[at] = held[code // blocks, :, pl.ds(start, width)]


def block_of(routed, at):
    return jnp.concatenate([part[at] for part in routed], 0)


def masked(tile, is_diag):
    size = tile.shape[0]
    row = lax.broadcasted_iota(jnp.int32, (size, size), 0)
    col = lax.broadcasted_iota(jnp.int32, (size, size), 1)
    return jnp.where((row == col) & (is_diag == 1), 0.0, tile)


def fetch_tiles(tiles, held, sem):
    copies = [
        pltpu.make_async_copy(tiles.at[at], held.at[at], sem.at[at]) for at in range(tiles.shape[0])
    ]
    for copy in copies:
        copy.start()


def tile_kernel(is_diag, tiles, after, high, low, held, sem):
    fetch_tiles(tiles, held, sem)

    def convert(at, carry):
        pltpu.make_async_copy(tiles.at[at], held.at[at], sem.at[at]).wait()
        high[at], low[at] = split(masked(held[at], is_diag[at]), 2)
        return carry

    lax.fori_loop(0, tiles.shape[0], convert, 0)


def product_kernel(x_count, row_local, place, tile_hi, tile_lo, *refs):
    routed, (keep, give, total) = refs[:-3], refs[-3:]
    blocks, samples, block = total.shape
    total[...] = jnp.zeros_like(total)

    def multiply(at, carry):
        source_hi, source_lo = split(block_of(routed, at), 2)
        stacked = dot(jnp.concatenate([source_hi, source_lo], 0), tile_hi[at], NT)
        product = stacked[:samples] + (stacked[samples:] + dot(source_hi, tile_lo[at], NT))
        total[row_local[at]] += product
        return carry

    lax.fori_loop(0, tile_hi.shape[0], multiply, 0)
    half = keep.shape[1] // 2
    for out, core in ((keep, place[4]), (give, 1 - place[4])):
        for dx in range(x_count):
            for du in range(2):
                source = (du * 2 + (place[2] ^ core)) * x_count + (x_count - dx) % x_count
                start = pl.multiple_of(source * half, half)
                for at in range(blocks):
                    out[dx, du * half : (du + 1) * half, at * block : (at + 1) * block] = total[
                        at, pl.ds(start, half), :
                    ]


def applied_kernel(count, *refs):
    keep, got, residual, diagonal = refs[:4]
    arrived = refs[4 : 4 + count]
    whole, first, second = refs[4 + count :]
    half = first.shape[0]
    value = keep[0] + got[0]
    for other in arrived:
        value = value + other[...]
    value = value + diagonal[...] * residual[...]
    whole[...] = value
    first[...] = value[:half]
    second[...] = value[half:]


def place_rows(x_count, place, parts, rows):
    half = parts[0].shape[0] // 2
    for dk in range(2):
        for dx in range(x_count):
            for du in range(2):
                target = (du * 2 + (place[2] ^ place[4] ^ dk)) * x_count + dx
                start = pl.multiple_of(target * half, half)
                rows[pl.ds(start, half)] = parts[dk * x_count + dx][du * half : (du + 1) * half]


def left_operand(rows, scale):
    high, low = split((rows * scale).T, 2)
    return jnp.concatenate([high, high, low], 1)


def right_operand(rows):
    high, low = split(rows, 2)
    return jnp.concatenate([high, low, high], 0)


def row_kernel(x_count, scale, place, after, *refs):
    parts, (rows, left) = refs[:-2], refs[-2:]
    place_rows(x_count, place, parts, rows)
    block = left.shape[1]
    for at in range(left.shape[0]):
        left[at] = left_operand(rows[:, at * block : (at + 1) * block], scale)


def first_kernel(x_count, scale, row_local, place, tiles, diagonal, resid_rows, after, *refs):
    inputs, (partial, new_diagonal, rows, left, sem) = refs[:-5], refs[-5:]
    parts, routed = inputs[: 2 * x_count], inputs[2 * x_count :]
    fetch_tiles(tiles, partial, sem)
    samples = rows.shape[0]
    block = left.shape[1]
    place_rows(x_count, place, parts, rows)
    for at in range(left.shape[0]):
        left[at] = left_operand(rows[:, at * block : (at + 1) * block], scale)
    stat = jnp.sum(rows[...] * resid_rows[...], axis=0, keepdims=True) / samples
    new_diagonal[...] = diagonal[...] - step_size * (stat - 1.0 / diagonal[...])

    def subtract(at, carry):
        right = right_operand(block_of(routed, at))
        term = dot(left[row_local[at]], right, NN)
        pltpu.make_async_copy(tiles.at[at], partial.at[at], sem.at[at]).wait()
        partial[at] = partial[at] + term
        return carry

    lax.fori_loop(0, tiles.shape[0], subtract, 0)


def last_kernel(row_local, is_diag, left, partial, *refs):
    routed, (new_tiles, held, sem) = refs[:-3], refs[-3:]
    bound = step_size * penalty

    def finish(at, carry):
        right = right_operand(block_of(routed, at))
        stepped = partial[at] + dot(left[row_local[at]], right, NN)
        held[at] = stepped - jnp.clip(stepped, -bound, bound)

        @pl.when(is_diag[at] == 1)
        def _():
            held[at] = masked(held[at], 1)

        pltpu.make_async_copy(held.at[at], new_tiles.at[at], sem.at[at]).start()
        return carry

    lax.fori_loop(0, partial.shape[0], finish, 0)
    for at in range(partial.shape[0]):
        pltpu.make_async_copy(held.at[at], new_tiles.at[at], sem.at[at]).wait()


def per_device(samples, loadings, omega_tiles, omega_diagonal, tile_rows, tile_cols):
    f32 = jnp.float32
    a_count, x_count = lax.axis_size("a"), lax.axis_size("x")
    row_count, col_count = 4 * a_count, 2 * x_count
    a, u, v, x, k = (lax.axis_index(name) for name in ROWS + COLS)
    sample_dev, var_dev = samples.shape
    half = sample_dev // 2
    sample_all = sample_dev * col_count
    factors = loadings.shape[0]
    tile_dev, block_size = omega_tiles.shape[:2]
    blocks_dev = var_dev // block_size
    plane = 4 * x_count
    hbm = pl.BlockSpec(memory_space=pltpu.HBM)
    vmem = pl.BlockSpec(memory_space=pltpu.VMEM)
    def cost(flops, moved):
        return pl.CostEstimate(flops=flops, bytes_accessed=moved, transcendentals=0)

    shape = lambda *dims: jax.ShapeDtypeStruct(dims, f32)

    place = jnp.stack([a, u, v, x, k]).astype(jnp.int32)
    def permute(value, names, target):
        sizes = [lax.axis_size(name) for name in names]

        def flat(coords):
            at = 0
            for coord, size in zip(coords, sizes):
                at = at * size + coord
            return at

        def coords_of(at):
            coords = []
            for size in reversed(sizes):
                coords.append(at % size)
                at //= size
            return tuple(reversed(coords))

        total = 1
        for size in sizes:
            total *= size
        return lax.ppermute(
            value, names, [(at, flat(target(*coords_of(at)))) for at in range(total)]
        )

    def swap_core(value):
        return permute(value, ("k",), lambda k: (1 - k,))

    def shift_x(value, dx):
        return permute(value, ("x",), lambda x: ((x + dx) % x_count,))

    def call(kernel, name, outs, operands, scratch=(), limit=24, estimate=None):
        arrays, specs = [], []
        for array, spec in operands:
            if spec is vmem:
                array = pltpu.with_memory_space_constraint(array, pltpu.VMEM)
            if spec is hbm:
                array = pltpu.with_memory_space_constraint(array, pltpu.HBM)
            arrays.append(array)
            specs.append(spec)
        return pl.pallas_call(
            kernel,
            out_shape=[out for out, _ in outs],
            in_specs=specs,
            out_specs=[spec for _, spec in outs],
            scratch_shapes=list(scratch),
            compiler_params=pltpu.CompilerParams(vmem_limit_bytes=limit * 1024 * 1024),
            cost_estimate=estimate,
            name=name,
        )(*arrays)

    def chip(dims, dtype=f32):
        return (pltpu.VMEM(dims, dtype), vmem)

    smem = pl.BlockSpec(memory_space=pltpu.SMEM)
    bf16 = jnp.bfloat16
    diagonal = omega_diagonal.reshape(1, var_dev)
    depth = 3 * sample_all
    tile_elements = tile_dev * block_size * block_size
    tile_sem = pltpu.SemaphoreType.DMA((tile_dev,))
    tile_shape = omega_tiles.shape
    scale = -step_size * 0.5 / sample_all
    field_outs = [chip((sample_dev, var_dev)), chip((half, var_dev)), chip((half, var_dev))]

    score_copies, held_samples, held_loadings = call(
        score_kernel,
        "scores",
        [
            chip((row_count, sample_dev, factors)),
            chip(samples.shape),
            chip(loadings.shape, bf16),
        ],
        [(samples, hbm), (loadings, hbm)],
        [pltpu.SemaphoreType.DMA((5,))],
    )
    score_terms = lax.all_to_all(score_copies, ROWS, 0, 0, tiled=True)
    row_local, is_diag, slot_index = call(
        functools.partial(table_kernel, (x_count, blocks_dev)),
        "tables",
        [
            (jax.ShapeDtypeStruct((count,), jnp.int32), smem)
            for count in (tile_dev, tile_dev, plane * tile_dev)
        ],
        [(place, smem), (tile_rows, smem), (tile_cols, smem), (score_copies, vmem)],
    )
    residual, resid_near, resid_far = call(
        residual_kernel,
        "residual",
        field_outs,
        [
            (place, smem),
            (score_terms, vmem),
            (held_samples, vmem),
            (held_loadings, vmem),
            (slot_index, smem),
        ],
    )

    def own_rows(whole):
        parts = [whole] + [shift_x(whole, dx) for dx in range(1, x_count)]
        return parts + [swap_core(part) for part in parts]

    def route(near, far, whole):
        held = [None] * (2 * a_count)
        for da in reversed(range(a_count)):
            for dz, part in ((1, far), (0, near)):
                held[da * 2 + dz] = permute(
                    part,
                    ("a", "u", "v", "k"),
                    lambda a, u, v, k: ((a + da) % a_count, u ^ dz, k, v),
                )
        beside = own_rows(whole)
        sources = []
        for part in held:
            sources += [part, swap_core(part)]
        slots = call(
            functools.partial(gather_kernel, len(sources), plane),
            "gather_slots",
            [chip((tile_dev, half, block_size))] * plane,
            [(slot_index, smem)] + [(part, vmem) for part in sources + beside],
            [pltpu.VMEM((len(sources), half, var_dev), f32)],
        )
        return slots, beside

    def deliver(slots):
        peers = {
            at: (at // (2 * x_count), (at // x_count) % 2, at % x_count) for at in range(plane)
        }
        routed = list(slots)
        for at in sorted(peers, key=lambda at: -sum(step > 0 for step in peers[at])):
            du, dv, dx = peers[at]
            if at > 0:
                routed[at] = permute(
                    slots[at], PLANE, lambda u, v, x: (u ^ du, v ^ dv, (x + dx) % x_count)
                )
        return routed

    resid_slots, resid_parts = route(resid_near, resid_far, residual)
    routed_resid = deliver(resid_slots)
    tiles_hi, tiles_lo = call(
        tile_kernel,
        "split_tiles",
        [chip(tile_shape, bf16), chip(tile_shape, bf16)],
        [(is_diag, smem), (omega_tiles, hbm), (resid_slots[0], vmem)],
        [pltpu.VMEM(tile_shape, f32), tile_sem],
        estimate=cost(0, 8 * tile_elements),
    )
    resid_rows, resid_left = call(
        functools.partial(row_kernel, x_count, scale),
        "resid_rows",
        [chip((sample_all, var_dev)), chip((blocks_dev, block_size, depth), bf16)],
        [(place, smem), (resid_slots[0], vmem)] + [(part, vmem) for part in resid_parts],
        estimate=cost(0, 16 * sample_all * var_dev),
    )

    keep, give = call(
        functools.partial(product_kernel, x_count),
        "products",
        [chip((x_count, sample_dev, var_dev))] * 2,
        [
            (row_local, smem),
            (place, smem),
            (tiles_hi, vmem),
            (tiles_lo, vmem),
        ]
        + [(part, vmem) for part in routed_resid],
        [pltpu.VMEM((blocks_dev, sample_all, block_size), f32)],
    )
    got = swap_core(give)
    arrived = [shift_x(keep[dx] + got[dx], dx) for dx in range(1, x_count)]
    applied, applied_near, applied_far = call(
        functools.partial(applied_kernel, len(arrived)),
        "applied",
        field_outs,
        [(part, vmem) for part in (keep, got, residual, diagonal, *arrived)],
    )

    applied_slots, applied_parts = route(applied_near, applied_far, applied)
    routed_applied = deliver(applied_slots)
    partial, new_diagonal = call(
        functools.partial(first_kernel, x_count, scale),
        "first_term",
        [chip(tile_shape), (shape(1, var_dev), vmem)],
        [
            (row_local, smem),
            (place, smem),
            (omega_tiles, hbm),
            (diagonal, vmem),
            (resid_rows, vmem),
            (applied_slots[0], vmem),
        ]
        + [(part, vmem) for part in applied_parts + routed_resid],
        [
            pltpu.VMEM((sample_all, var_dev), f32),
            pltpu.VMEM((blocks_dev, block_size, depth), bf16),
            tile_sem,
        ],
        estimate=cost(2 * depth * tile_elements, 16 * tile_elements),
    )
    (new_tiles,) = call(
        last_kernel,
        "last_term",
        [(shape(*tile_shape), hbm)],
        [
            (row_local, smem),
            (is_diag, smem),
            (resid_left, vmem),
            (partial, vmem),
        ]
        + [(part, vmem) for part in routed_applied],
        [pltpu.VMEM(tile_shape, f32), tile_sem],
    )
    return new_tiles, new_diagonal.reshape(var_dev)


def solution(mesh):
    rows, cols = mesh.shape["rows"], mesh.shape["cols"]
    fine = Mesh(mesh.devices.reshape(rows // 4, 2, 2, cols // 2, 2), ROWS + COLS)
    placed = (
        P(COLS, ROWS),
        P(None, ROWS),
        P(ROWS + COLS, None, None),
        P(ROWS),
        P(),
        P(),
    )
    return jax.shard_map(
        per_device,
        mesh=fine,
        in_specs=placed,
        out_specs=(P(ROWS + COLS, None, None), P(ROWS)),
        check_vma=False,
    )
```

```python
import functools

import jax
import jax.numpy as jnp
from jax import lax
from jax.experimental import pallas as pl
from jax.experimental.pallas import tpu as pltpu
from jax.sharding import Mesh
from jax.sharding import PartitionSpec as P

step_size = 0.5
penalty = 0.02

ROWS = ("a", "u", "v")
COLS = ("x", "k")
PLANE = ("u", "v", "x")


def exchange_order(a_count):
    return [(da, dz) for da in reversed(range(a_count)) for dz in (1, 0)]


def plane_order(x_count):
    steps = [(du, dv, dx) for du in range(2) for dv in range(2) for dx in range(x_count)]
    return sorted(steps[1:], key=lambda step: -sum(part > 0 for part in step))


NT = (((1,), (1,)), ((), ()))
NN = (((1,), (0,)), ((), ()))


def dot(left, right, dims):
    return lax.dot_general(left, right, dims, preferred_element_type=jnp.float32)


def split(value, pieces):
    found = []
    for _ in range(pieces):
        piece = value.astype(jnp.bfloat16)
        found.append(piece)
        value = value - piece.astype(jnp.float32)
    return found


def table_kernel(sizes, place, tile_rows, tile_cols, after, row_local, is_diag, slot_index):
    x_count, blocks = sizes
    a, u, v, x, k = (place[at] for at in range(5))
    tile_dev = row_local.shape[0]

    def first_tile(u, v, x):
        return ((((a * 2 + u) * 2 + v) * x_count + x) * 2 + k) * tile_dev

    mine = first_tile(u, v, x)
    for at in range(tile_dev):
        row, col = tile_rows[mine + at], tile_cols[mine + at]
        row_local[at] = row - ((a * 2 + u) * 2 + v) * blocks
        is_diag[at] = jnp.where(row == col, 1, 0)
    a_count = tile_cols.shape[0] // (8 * x_count * tile_dev)
    peer = 0
    for du in range(2):
        for dv in range(2):
            for dx in range(x_count):
                theirs = first_tile(u ^ du, v ^ dv, lax.rem(x + dx, x_count))
                for at in range(tile_dev):
                    col = tile_cols[theirs + at]
                    group = col // blocks
                    da = lax.rem(a + a_count - group // 4, a_count)
                    part = (da * 2 + (((group // 2) % 2) ^ u)) * 2 + ((group % 2) ^ k)
                    slot_index[peer * tile_dev + at] = part * blocks + col % blocks
                peer += 1


def score_kernel(samples, loadings, out, held_samples, held, sem):
    rows, variables = samples.shape
    chunks = sem.shape[0] - 1
    width = variables // chunks
    whole = pltpu.make_async_copy(samples, held_samples, sem.at[chunks])
    whole.start()
    copies = [
        pltpu.make_async_copy(
            loadings.at[:, at * width : (at + 1) * width],
            held.at[:, at * width : (at + 1) * width],
            sem.at[at],
        )
        for at in range(chunks)
    ]
    for copy in copies:
        copy.start()
    whole.wait()
    found = None
    for at, copy in enumerate(copies):
        here = slice(at * width, (at + 1) * width)
        pieces = jnp.concatenate(split(held_samples[:, here], 3), 0)
        copy.wait()
        term = dot(pieces, held[:, here], NT)
        found = term if found is None else found + term
    value = (found[2 * rows :] + found[rows : 2 * rows]) + found[:rows]
    for copy in range(out.shape[0]):
        out[copy] = value


def residual_kernel(place, scores, samples, loadings, after, whole, first, second):
    rows, variables = samples.shape
    half = rows // 2
    value = scores[0]
    for source in range(1, scores.shape[0]):
        value = value + scores[source]
    pieces = jnp.concatenate(split(value, 3), 0)
    upper = place[1] == 1
    width = variables // 4
    for at in range(0, variables, width):
        here = slice(at, at + width)
        fitted = dot(pieces, loadings[:, here], NN)
        value = samples[:, here] - ((fitted[2 * rows :] + fitted[rows : 2 * rows]) + fitted[:rows])
        low, high = value[:half], value[half:]
        near = jnp.where(upper, high, low)
        far = jnp.where(upper, low, high)
        whole[:half, here] = near
        whole[half:, here] = far
        first[:, here] = near
        second[:, here] = far


def gather_kernel(count, peers, index, *refs):
    sources, outs, held = refs[:count], refs[-1 - peers : -1], refs[-1]
    for at, source in enumerate(sources):
        held[at] = source[...]
    tile_dev, _, width = outs[0].shape
    blocks = held.shape[2] // width
    for peer, out in enumerate(outs):
        for at in range(tile_dev):
            code = index[peer * tile_dev + at]
            start = pl.multiple_of((code % blocks) * width, width)
            out[at] = held[code // blocks, :, pl.ds(start, width)]


def block_of(routed, at):
    return jnp.concatenate([part[at] for part in routed], 0)


def masked(tile, is_diag):
    size = tile.shape[0]
    row = lax.broadcasted_iota(jnp.int32, (size, size), 0)
    col = lax.broadcasted_iota(jnp.int32, (size, size), 1)
    return jnp.where((row == col) & (is_diag == 1), 0.0, tile)


def fetch_tiles(tiles, held, sem):
    copies = [
        pltpu.make_async_copy(tiles.at[at], held.at[at], sem.at[at]) for at in range(tiles.shape[0])
    ]
    for copy in copies:
        copy.start()


def tile_kernel(is_diag, tiles, after, high, low, held, sem):
    fetch_tiles(tiles, held, sem)

    def convert(at, carry):
        pltpu.make_async_copy(tiles.at[at], held.at[at], sem.at[at]).wait()
        high[at], low[at] = split(masked(held[at], is_diag[at]), 2)
        return carry

    lax.fori_loop(0, tiles.shape[0], convert, 0)


def product_kernel(x_count, row_local, place, tile_hi, tile_lo, *refs):
    routed, (keep, give, total) = refs[:-3], refs[-3:]
    blocks, samples, block = total.shape
    total[...] = jnp.zeros_like(total)

    def multiply(at, carry):
        source_hi, source_lo = split(block_of(routed, at), 2)
        stacked = dot(jnp.concatenate([source_hi, source_lo], 0), tile_hi[at], NT)
        product = stacked[:samples] + (stacked[samples:] + dot(source_hi, tile_lo[at], NT))
        total[row_local[at]] += product
        return carry

    lax.fori_loop(0, tile_hi.shape[0], multiply, 0)
    half = keep.shape[1] // 2
    for out, core in ((keep, place[4]), (give, 1 - place[4])):
        for dx in range(x_count):
            for du in range(2):
                source = (du * 2 + (place[2] ^ core)) * x_count + (x_count - dx) % x_count
                start = pl.multiple_of(source * half, half)
                for at in range(blocks):
                    out[dx, du * half : (du + 1) * half, at * block : (at + 1) * block] = total[
                        at, pl.ds(start, half), :
                    ]


def applied_kernel(count, *refs):
    keep, got, residual, diagonal = refs[:4]
    arrived = refs[4 : 4 + count]
    whole, first, second = refs[4 + count :]
    half = first.shape[0]
    value = keep[0] + got[0]
    for other in arrived:
        value = value + other[...]
    value = value + diagonal[...] * residual[...]
    whole[...] = value
    first[...] = value[:half]
    second[...] = value[half:]


def place_rows(x_count, place, parts, rows):
    half = parts[0].shape[0] // 2
    for dk in range(2):
        for dx in range(x_count):
            for du in range(2):
                target = (du * 2 + (place[2] ^ place[4] ^ dk)) * x_count + dx
                start = pl.multiple_of(target * half, half)
                rows[pl.ds(start, half)] = parts[dk * x_count + dx][du * half : (du + 1) * half]


def left_operand(rows, scale):
    high, low = split((rows * scale).T, 2)
    return jnp.concatenate([high, high, low], 1)


def right_operand(rows):
    high, low = split(rows, 2)
    return jnp.concatenate([high, low, high], 0)


def row_kernel(x_count, scale, place, after, *refs):
    parts, (rows, left) = refs[:-2], refs[-2:]
    place_rows(x_count, place, parts, rows)
    block = left.shape[1]
    for at in range(left.shape[0]):
        left[at] = left_operand(rows[:, at * block : (at + 1) * block], scale)


def first_kernel(x_count, scale, row_local, place, tiles, diagonal, resid_rows, after, *refs):
    inputs, (partial, new_diagonal, rows, left, sem) = refs[:-5], refs[-5:]
    parts, routed = inputs[: 2 * x_count], inputs[2 * x_count :]
    fetch_tiles(tiles, partial, sem)
    samples = rows.shape[0]
    block = left.shape[1]
    place_rows(x_count, place, parts, rows)
    for at in range(left.shape[0]):
        left[at] = left_operand(rows[:, at * block : (at + 1) * block], scale)
    stat = jnp.sum(rows[...] * resid_rows[...], axis=0, keepdims=True) / samples
    new_diagonal[...] = diagonal[...] - step_size * (stat - 1.0 / diagonal[...])

    def subtract(at, carry):
        right = right_operand(block_of(routed, at))
        term = dot(left[row_local[at]], right, NN)
        pltpu.make_async_copy(tiles.at[at], partial.at[at], sem.at[at]).wait()
        partial[at] = partial[at] + term
        return carry

    lax.fori_loop(0, tiles.shape[0], subtract, 0)


def last_kernel(row_local, is_diag, left, partial, *refs):
    routed, (new_tiles, held, sem) = refs[:-3], refs[-3:]
    bound = step_size * penalty

    def finish(at, carry):
        right = right_operand(block_of(routed, at))
        stepped = partial[at] + dot(left[row_local[at]], right, NN)
        held[at] = stepped - jnp.clip(stepped, -bound, bound)

        @pl.when(is_diag[at] == 1)
        def _():
            held[at] = masked(held[at], 1)

        pltpu.make_async_copy(held.at[at], new_tiles.at[at], sem.at[at]).start()
        return carry

    lax.fori_loop(0, partial.shape[0], finish, 0)
    for at in range(partial.shape[0]):
        pltpu.make_async_copy(held.at[at], new_tiles.at[at], sem.at[at]).wait()


def per_device(samples, loadings, omega_tiles, omega_diagonal, tile_rows, tile_cols):
    f32 = jnp.float32
    a_count, x_count = lax.axis_size("a"), lax.axis_size("x")
    row_count, col_count = 4 * a_count, 2 * x_count
    a, u, v, x, k = (lax.axis_index(name) for name in ROWS + COLS)
    sample_dev, var_dev = samples.shape
    half = sample_dev // 2
    sample_all = sample_dev * col_count
    factors = loadings.shape[0]
    tile_dev, block_size = omega_tiles.shape[:2]
    blocks_dev = var_dev // block_size
    plane = 4 * x_count
    hbm = pl.BlockSpec(memory_space=pltpu.HBM)
    vmem = pl.BlockSpec(memory_space=pltpu.VMEM)

    def cost(flops, moved):
        return pl.CostEstimate(flops=flops, bytes_accessed=moved, transcendentals=0)

    shape = lambda *dims: jax.ShapeDtypeStruct(dims, f32)

    place = jnp.stack([a, u, v, x, k]).astype(jnp.int32)

    def permute(value, names, target):
        sizes = [lax.axis_size(name) for name in names]

        def flat(coords):
            at = 0
            for coord, size in zip(coords, sizes):
                at = at * size + coord
            return at

        def coords_of(at):
            coords = []
            for size in reversed(sizes):
                coords.append(at % size)
                at //= size
            return tuple(reversed(coords))

        total = 1
        for size in sizes:
            total *= size
        return lax.ppermute(
            value, names, [(at, flat(target(*coords_of(at)))) for at in range(total)]
        )

    def swap_core(value):
        return permute(value, ("k",), lambda k: (1 - k,))

    def shift_x(value, dx):
        return permute(value, ("x",), lambda x: ((x + dx) % x_count,))

    def call(kernel, outs, operands, scratch=(), limit=24, estimate=None):
        arrays, specs = [], []
        for array, spec in operands:
            if spec is vmem:
                array = pltpu.with_memory_space_constraint(array, pltpu.VMEM)
            if spec is hbm:
                array = pltpu.with_memory_space_constraint(array, pltpu.HBM)
            arrays.append(array)
            specs.append(spec)
        return pl.pallas_call(
            kernel,
            out_shape=[out for out, _ in outs],
            in_specs=specs,
            out_specs=[spec for _, spec in outs],
            scratch_shapes=list(scratch),
            compiler_params=pltpu.CompilerParams(vmem_limit_bytes=limit * 1024 * 1024),
            cost_estimate=estimate,
        )(*arrays)

    def chip(dims, dtype=f32):
        return (pltpu.VMEM(dims, dtype), vmem)

    smem = pl.BlockSpec(memory_space=pltpu.SMEM)
    bf16 = jnp.bfloat16
    diagonal = omega_diagonal.reshape(1, var_dev)
    depth = 3 * sample_all
    tile_elements = tile_dev * block_size * block_size
    tile_sem = pltpu.SemaphoreType.DMA((tile_dev,))
    tile_shape = omega_tiles.shape
    scale = -step_size * 0.5 / sample_all
    field_outs = [chip((sample_dev, var_dev)), chip((half, var_dev)), chip((half, var_dev))]

    score_copies, held_samples, held_loadings = call(
        score_kernel,
        [
            chip((row_count, sample_dev, factors)),
            chip(samples.shape),
            chip(loadings.shape, bf16),
        ],
        [(samples, hbm), (loadings, hbm)],
        [pltpu.SemaphoreType.DMA((5,))],
    )
    score_terms = lax.all_to_all(score_copies, ROWS, 0, 0, tiled=True)
    row_local, is_diag, slot_index = call(
        functools.partial(table_kernel, (x_count, blocks_dev)),
        [
            (jax.ShapeDtypeStruct((count,), jnp.int32), smem)
            for count in (tile_dev, tile_dev, plane * tile_dev)
        ],
        [(place, smem), (tile_rows, smem), (tile_cols, smem), (score_copies, vmem)],
    )
    residual, resid_near, resid_far = call(
        residual_kernel,
        field_outs,
        [
            (place, smem),
            (score_terms, vmem),
            (held_samples, vmem),
            (held_loadings, vmem),
            (slot_index, smem),
        ],
    )

    def own_rows(whole):
        parts = [whole]
        for dx in range(1, x_count):
            parts.append(shift_x(whole, dx))
        return parts + [swap_core(part) for part in parts]

    def route(near, far, whole):
        held = [None] * (2 * a_count)
        for da, dz in exchange_order(a_count):
            held[da * 2 + dz] = permute(
                far if dz else near,
                ("a", "u", "v", "k"),
                lambda a, u, v, k: ((a + da) % a_count, u ^ dz, k, v),
            )
        beside = own_rows(whole)
        sources = []
        for part in held:
            sources += [part, swap_core(part)]
        slots = call(
            functools.partial(gather_kernel, len(sources), plane),
            [chip((tile_dev, half, block_size))] * plane,
            [(slot_index, smem)] + [(part, vmem) for part in sources + beside],
            [pltpu.VMEM((len(sources), half, var_dev), f32)],
        )
        return slots, beside

    def deliver(slots):
        routed = list(slots)
        for du, dv, dx in plane_order(x_count):
            at = (du * 2 + dv) * x_count + dx
            routed[at] = permute(
                slots[at], PLANE, lambda u, v, x: (u ^ du, v ^ dv, (x + dx) % x_count)
            )
        return routed

    resid_slots, resid_parts = route(resid_near, resid_far, residual)
    routed_resid = deliver(resid_slots)
    tiles_hi, tiles_lo = call(
        tile_kernel,
        [chip(tile_shape, bf16), chip(tile_shape, bf16)],
        [(is_diag, smem), (omega_tiles, hbm), (resid_slots[0], vmem)],
        [pltpu.VMEM(tile_shape, f32), tile_sem],
        estimate=cost(0, 8 * tile_elements),
    )
    resid_rows, resid_left = call(
        functools.partial(row_kernel, x_count, scale),
        [chip((sample_all, var_dev)), chip((blocks_dev, block_size, depth), bf16)],
        [(place, smem), (resid_slots[0], vmem)] + [(part, vmem) for part in resid_parts],
        estimate=cost(0, 16 * sample_all * var_dev),
    )

    keep, give = call(
        functools.partial(product_kernel, x_count),
        [chip((x_count, sample_dev, var_dev))] * 2,
        [
            (row_local, smem),
            (place, smem),
            (tiles_hi, vmem),
            (tiles_lo, vmem),
        ]
        + [(part, vmem) for part in routed_resid],
        [pltpu.VMEM((blocks_dev, sample_all, block_size), f32)],
    )
    got = swap_core(give)
    arrived = [shift_x(keep[dx] + got[dx], dx) for dx in range(1, x_count)]
    applied, applied_near, applied_far = call(
        functools.partial(applied_kernel, len(arrived)),
        field_outs,
        [(part, vmem) for part in (keep, got, residual, diagonal, *arrived)],
    )

    applied_slots, applied_parts = route(applied_near, applied_far, applied)
    routed_applied = deliver(applied_slots)
    partial, new_diagonal = call(
        functools.partial(first_kernel, x_count, scale),
        [chip(tile_shape), (shape(1, var_dev), vmem)],
        [
            (row_local, smem),
            (place, smem),
            (omega_tiles, hbm),
            (diagonal, vmem),
            (resid_rows, vmem),
            (applied_slots[0], vmem),
        ]
        + [(part, vmem) for part in applied_parts + routed_resid],
        [
            pltpu.VMEM((sample_all, var_dev), f32),
            pltpu.VMEM((blocks_dev, block_size, depth), bf16),
            tile_sem,
        ],
        estimate=cost(2 * depth * tile_elements, 16 * tile_elements),
    )
    (new_tiles,) = call(
        last_kernel,
        [(shape(*tile_shape), hbm)],
        [
            (row_local, smem),
            (is_diag, smem),
            (resid_left, vmem),
            (partial, vmem),
        ]
        + [(part, vmem) for part in routed_applied],
        [pltpu.VMEM(tile_shape, f32), tile_sem],
    )
    return new_tiles, new_diagonal.reshape(var_dev)


def solution(mesh):
    rows, cols = mesh.shape["rows"], mesh.shape["cols"]
    fine = Mesh(mesh.devices.reshape(rows // 4, 2, 2, cols // 2, 2), ROWS + COLS)
    placed = (
        P(COLS, ROWS),
        P(None, ROWS),
        P(ROWS + COLS, None, None),
        P(ROWS),
        P(),
        P(),
    )
    return jax.shard_map(
        per_device,
        mesh=fine,
        in_specs=placed,
        out_specs=(P(ROWS + COLS, None, None), P(ROWS)),
        check_vma=False,
    )
```

```python
import functools

import jax
import jax.numpy as jnp
from jax import lax
from jax.experimental import pallas as pl
from jax.experimental.pallas import tpu as pltpu
from jax.sharding import Mesh
from jax.sharding import PartitionSpec as P

step_size = 0.5
penalty = 0.02

ROWS = ("a", "u", "v")
COLS = ("x", "k")
PLANE = ("u", "v", "x")


def plane_order(x_count):
    steps = [(du, dv, dx) for du in range(2) for dv in range(2) for dx in range(x_count)]
    return sorted(steps[1:], key=lambda step: -sum(part > 0 for part in step))


NT = (((1,), (1,)), ((), ()))
NN = (((1,), (0,)), ((), ()))


def dot(left, right, dims):
    return lax.dot_general(left, right, dims, preferred_element_type=jnp.float32)


def split(value, pieces):
    found = []
    for _ in range(pieces):
        piece = value.astype(jnp.bfloat16)
        found.append(piece)
        value = value - piece.astype(jnp.float32)
    return found


def table_kernel(sizes, place, tile_rows, tile_cols, after, row_local, is_diag, slot_index):
    x_count, blocks = sizes
    a, u, v, x, k = (place[at] for at in range(5))
    tile_dev = row_local.shape[0]

    def first_tile(u, v, x):
        return ((((a * 2 + u) * 2 + v) * x_count + x) * 2 + k) * tile_dev

    mine = first_tile(u, v, x)
    for at in range(tile_dev):
        row, col = tile_rows[mine + at], tile_cols[mine + at]
        row_local[at] = row - ((a * 2 + u) * 2 + v) * blocks
        is_diag[at] = jnp.where(row == col, 1, 0)
    a_count = tile_cols.shape[0] // (8 * x_count * tile_dev)
    peer = 0
    for du in range(2):
        for dv in range(2):
            for dx in range(x_count):
                theirs = first_tile(u ^ du, v ^ dv, lax.rem(x + dx, x_count))
                for at in range(tile_dev):
                    col = tile_cols[theirs + at]
                    group = col // blocks
                    da = lax.rem(a + a_count - group // 4, a_count)
                    part = (da * 2 + (((group // 2) % 2) ^ u)) * 2 + ((group % 2) ^ k)
                    slot_index[peer * tile_dev + at] = part * blocks + col % blocks
                peer += 1


def score_kernel(samples, loadings, out, held_samples, held, sem):
    rows, variables = samples.shape
    chunks = sem.shape[0] - 1
    width = variables // chunks
    whole = pltpu.make_async_copy(samples, held_samples, sem.at[chunks])
    whole.start()
    copies = [
        pltpu.make_async_copy(
            loadings.at[:, at * width : (at + 1) * width],
            held.at[:, at * width : (at + 1) * width],
            sem.at[at],
        )
        for at in range(chunks)
    ]
    for copy in copies:
        copy.start()
    whole.wait()
    found = None
    for at, copy in enumerate(copies):
        here = slice(at * width, (at + 1) * width)
        pieces = jnp.concatenate(split(held_samples[:, here], 3), 0)
        copy.wait()
        term = dot(pieces, held[:, here], NT)
        found = term if found is None else found + term
    value = (found[2 * rows :] + found[rows : 2 * rows]) + found[:rows]
    for copy in range(out.shape[0]):
        out[copy] = value


def residual_kernel(place, scores, samples, loadings, after, whole, first, second):
    rows, variables = samples.shape
    half = rows // 2
    value = scores[0]
    for source in range(1, scores.shape[0]):
        value = value + scores[source]
    pieces = jnp.concatenate(split(value, 3), 0)
    upper = place[1] == 1
    width = variables // 4
    for at in range(0, variables, width):
        here = slice(at, at + width)
        fitted = dot(pieces, loadings[:, here], NN)
        value = samples[:, here] - ((fitted[2 * rows :] + fitted[rows : 2 * rows]) + fitted[:rows])
        low, high = value[:half], value[half:]
        near = jnp.where(upper, high, low)
        far = jnp.where(upper, low, high)
        whole[:half, here] = near
        whole[half:, here] = far
        first[:, here] = near
        second[:, here] = far


def gather_kernel(count, peers, index, *refs):
    sources, outs, held = refs[:count], refs[-1 - peers : -1], refs[-1]
    for at, source in enumerate(sources):
        held[at] = source[...]
    tile_dev, _, width = outs[0].shape
    blocks = held.shape[2] // width
    for peer, out in enumerate(outs):
        for at in range(tile_dev):
            code = index[peer * tile_dev + at]
            start = pl.multiple_of((code % blocks) * width, width)
            out[at] = held[code // blocks, :, pl.ds(start, width)]


def block_of(routed, at):
    return jnp.concatenate([part[at] for part in routed], 0)


def masked(tile, is_diag):
    size = tile.shape[0]
    row = lax.broadcasted_iota(jnp.int32, (size, size), 0)
    col = lax.broadcasted_iota(jnp.int32, (size, size), 1)
    return jnp.where((row == col) & (is_diag == 1), 0.0, tile)


def fetch_tiles(tiles, held, sem):
    copies = [
        pltpu.make_async_copy(tiles.at[at], held.at[at], sem.at[at]) for at in range(tiles.shape[0])
    ]
    for copy in copies:
        copy.start()


def tile_kernel(is_diag, tiles, after, high, low, held, sem):
    fetch_tiles(tiles, held, sem)

    def convert(at, carry):
        pltpu.make_async_copy(tiles.at[at], held.at[at], sem.at[at]).wait()
        high[at], low[at] = split(masked(held[at], is_diag[at]), 2)
        return carry

    lax.fori_loop(0, tiles.shape[0], convert, 0)


def product_kernel(x_count, row_local, place, tile_hi, tile_lo, *refs):
    routed, sides, total = refs[:-5], refs[-5:-1], refs[-1]
    blocks, samples, block = total.shape
    total[...] = jnp.zeros_like(total)

    def multiply(at, carry):
        source_hi, source_lo = split(block_of(routed, at), 2)
        stacked = dot(jnp.concatenate([source_hi, source_lo], 0), tile_hi[at], NT)
        product = stacked[:samples] + (stacked[samples:] + dot(source_hi, tile_lo[at], NT))
        total[row_local[at]] += product
        return carry

    lax.fori_loop(0, tile_hi.shape[0], multiply, 0)
    for side, out in enumerate(sides):
        du, core = side // 2, place[4] ^ (side % 2)
        half = out.shape[1]
        for dx in range(x_count):
            source = (du * 2 + (place[2] ^ core)) * x_count + (x_count - dx) % x_count
            start = pl.multiple_of(source * half, half)
            for at in range(blocks):
                out[dx, :, at * block : (at + 1) * block] = total[at, pl.ds(start, half), :]


def applied_kernel(du, count, *refs):
    keep, got, residual, diagonal = refs[:4]
    arrived = refs[4 : 4 + count]
    half = keep.shape[1]
    value = keep[0] + got[0]
    for other in arrived:
        value = value + other[...]
    value = value + diagonal[...] * residual[du * half : (du + 1) * half]
    if du == 0:
        refs[-1][...] = value
    else:
        earlier, part, whole = refs[-3:]
        part[...] = value
        whole[:half] = earlier[...]
        whole[half:] = value


def place_rows(x_count, place, parts, rows):
    half = parts[0].shape[0] // 2
    for dk in range(2):
        for dx in range(x_count):
            for du in range(2):
                target = (du * 2 + (place[2] ^ place[4] ^ dk)) * x_count + dx
                start = pl.multiple_of(target * half, half)
                rows[pl.ds(start, half)] = parts[dk * x_count + dx][du * half : (du + 1) * half]


def left_operand(rows, scale):
    high, low = split((rows * scale).T, 2)
    return jnp.concatenate([high, high, low], 1)


def right_operand(rows):
    high, low = split(rows, 2)
    return jnp.concatenate([high, low, high], 0)


def row_kernel(x_count, scale, place, after, *refs):
    parts, (rows, left) = refs[:-2], refs[-2:]
    place_rows(x_count, place, parts, rows)
    block = left.shape[1]
    for at in range(left.shape[0]):
        left[at] = left_operand(rows[:, at * block : (at + 1) * block], scale)


def first_kernel(x_count, scale, row_local, place, tiles, diagonal, resid_rows, after, *refs):
    inputs, (partial, new_diagonal, rows, left, sem) = refs[:-5], refs[-5:]
    parts, routed = inputs[: 2 * x_count], inputs[2 * x_count :]
    fetch_tiles(tiles, partial, sem)
    samples = rows.shape[0]
    block = left.shape[1]
    place_rows(x_count, place, parts, rows)
    for at in range(left.shape[0]):
        left[at] = left_operand(rows[:, at * block : (at + 1) * block], scale)
    stat = jnp.sum(rows[...] * resid_rows[...], axis=0, keepdims=True) / samples
    new_diagonal[...] = diagonal[...] - step_size * (stat - 1.0 / diagonal[...])

    def subtract(at, carry):
        right = right_operand(block_of(routed, at))
        term = dot(left[row_local[at]], right, NN)
        pltpu.make_async_copy(tiles.at[at], partial.at[at], sem.at[at]).wait()
        partial[at] = partial[at] + term
        return carry

    lax.fori_loop(0, tiles.shape[0], subtract, 0)


def last_kernel(row_local, is_diag, left, partial, *refs):
    routed, (new_tiles, held, sem) = refs[:-3], refs[-3:]
    bound = step_size * penalty

    def finish(at, carry):
        right = right_operand(block_of(routed, at))
        stepped = partial[at] + dot(left[row_local[at]], right, NN)
        held[at] = stepped - jnp.clip(stepped, -bound, bound)

        @pl.when(is_diag[at] == 1)
        def _():
            held[at] = masked(held[at], 1)

        pltpu.make_async_copy(held.at[at], new_tiles.at[at], sem.at[at]).start()
        return carry

    lax.fori_loop(0, partial.shape[0], finish, 0)
    for at in range(partial.shape[0]):
        pltpu.make_async_copy(held.at[at], new_tiles.at[at], sem.at[at]).wait()


def per_device(samples, loadings, omega_tiles, omega_diagonal, tile_rows, tile_cols):
    f32 = jnp.float32
    a_count, x_count = lax.axis_size("a"), lax.axis_size("x")
    row_count, col_count = 4 * a_count, 2 * x_count
    a, u, v, x, k = (lax.axis_index(name) for name in ROWS + COLS)
    sample_dev, var_dev = samples.shape
    half = sample_dev // 2
    sample_all = sample_dev * col_count
    factors = loadings.shape[0]
    tile_dev, block_size = omega_tiles.shape[:2]
    blocks_dev = var_dev // block_size
    plane = 4 * x_count
    hbm = pl.BlockSpec(memory_space=pltpu.HBM)
    vmem = pl.BlockSpec(memory_space=pltpu.VMEM)

    def cost(flops, moved):
        return pl.CostEstimate(flops=flops, bytes_accessed=moved, transcendentals=0)

    shape = lambda *dims: jax.ShapeDtypeStruct(dims, f32)

    place = jnp.stack([a, u, v, x, k]).astype(jnp.int32)

    def permute(value, names, target):
        sizes = [lax.axis_size(name) for name in names]

        def flat(coords):
            at = 0
            for coord, size in zip(coords, sizes):
                at = at * size + coord
            return at

        def coords_of(at):
            coords = []
            for size in reversed(sizes):
                coords.append(at % size)
                at //= size
            return tuple(reversed(coords))

        total = 1
        for size in sizes:
            total *= size
        return lax.ppermute(
            value, names, [(at, flat(target(*coords_of(at)))) for at in range(total)]
        )

    def swap_core(value):
        return permute(value, ("k",), lambda k: (1 - k,))

    def shift_x(value, dx):
        return permute(value, ("x",), lambda x: ((x + dx) % x_count,))

    def call(kernel, outs, operands, scratch=(), limit=24, estimate=None):
        arrays, specs = [], []
        for array, spec in operands:
            if spec is vmem:
                array = pltpu.with_memory_space_constraint(array, pltpu.VMEM)
            if spec is hbm:
                array = pltpu.with_memory_space_constraint(array, pltpu.HBM)
            arrays.append(array)
            specs.append(spec)
        return pl.pallas_call(
            kernel,
            out_shape=[out for out, _ in outs],
            in_specs=specs,
            out_specs=[spec for _, spec in outs],
            scratch_shapes=list(scratch),
            compiler_params=pltpu.CompilerParams(vmem_limit_bytes=limit * 1024 * 1024),
            cost_estimate=estimate,
        )(*arrays)

    def chip(dims, dtype=f32):
        return (pltpu.VMEM(dims, dtype), vmem)

    smem = pl.BlockSpec(memory_space=pltpu.SMEM)
    bf16 = jnp.bfloat16
    diagonal = omega_diagonal.reshape(1, var_dev)
    depth = 3 * sample_all
    tile_elements = tile_dev * block_size * block_size
    tile_sem = pltpu.SemaphoreType.DMA((tile_dev,))
    tile_shape = omega_tiles.shape
    scale = -step_size * 0.5 / sample_all
    field_outs = [chip((sample_dev, var_dev)), chip((half, var_dev)), chip((half, var_dev))]

    score_copies, held_samples, held_loadings = call(
        score_kernel,
        [
            chip((row_count, sample_dev, factors)),
            chip(samples.shape),
            chip(loadings.shape, bf16),
        ],
        [(samples, hbm), (loadings, hbm)],
        [pltpu.SemaphoreType.DMA((5,))],
    )
    score_terms = lax.all_to_all(score_copies, ROWS, 0, 0, tiled=True)
    row_local, is_diag, slot_index = call(
        functools.partial(table_kernel, (x_count, blocks_dev)),
        [
            (jax.ShapeDtypeStruct((count,), jnp.int32), smem)
            for count in (tile_dev, tile_dev, plane * tile_dev)
        ],
        [(place, smem), (tile_rows, smem), (tile_cols, smem), (score_copies, vmem)],
    )
    residual, resid_near, resid_far = call(
        residual_kernel,
        field_outs,
        [
            (place, smem),
            (score_terms, vmem),
            (held_samples, vmem),
            (held_loadings, vmem),
            (slot_index, smem),
        ],
    )

    def own_rows(whole):
        parts = [whole]
        for dx in range(1, x_count):
            parts.append(shift_x(whole, dx))
        return parts + [swap_core(part) for part in parts]

    def exchange(part, dz):
        held = [None] * a_count
        for da in reversed(range(a_count)):
            held[da] = permute(
                part,
                ("a", "u", "v", "k"),
                lambda a, u, v, k: ((a + da) % a_count, u ^ dz, k, v),
            )
        return [[arrived, swap_core(arrived)] for arrived in held]

    def gather_slots(near, far, beside):
        sources = [part for pair in zip(near, far) for parts in pair for part in parts]
        return call(
            functools.partial(gather_kernel, len(sources), plane),
            [chip((tile_dev, half, block_size))] * plane,
            [(slot_index, smem)] + [(part, vmem) for part in sources + beside],
            [pltpu.VMEM((len(sources), half, var_dev), f32)],
        )

    def deliver(slots):
        routed = list(slots)
        for du, dv, dx in plane_order(x_count):
            at = (du * 2 + dv) * x_count + dx
            routed[at] = permute(
                slots[at], PLANE, lambda u, v, x: (u ^ du, v ^ dv, (x + dx) % x_count)
            )
        return routed

    resid_parts = own_rows(residual)
    resid_slots = gather_slots(exchange(resid_near, 0), exchange(resid_far, 1), resid_parts)
    routed_resid = deliver(resid_slots)
    tiles_hi, tiles_lo = call(
        tile_kernel,
        [chip(tile_shape, bf16), chip(tile_shape, bf16)],
        [(is_diag, smem), (omega_tiles, hbm), (resid_slots[0], vmem)],
        [pltpu.VMEM(tile_shape, f32), tile_sem],
        estimate=cost(0, 8 * tile_elements),
    )
    resid_rows, resid_left = call(
        functools.partial(row_kernel, x_count, scale),
        [chip((sample_all, var_dev)), chip((blocks_dev, block_size, depth), bf16)],
        [(place, smem), (resid_slots[0], vmem)] + [(part, vmem) for part in resid_parts],
        estimate=cost(0, 16 * sample_all * var_dev),
    )

    sides = call(
        functools.partial(product_kernel, x_count),
        [chip((x_count, half, var_dev))] * 4,
        [
            (row_local, smem),
            (place, smem),
            (tiles_hi, vmem),
            (tiles_lo, vmem),
        ]
        + [(part, vmem) for part in routed_resid],
        [pltpu.VMEM((blocks_dev, sample_all, block_size), f32)],
    )
    halves, exchanged = [], []
    for du in range(2):
        keep, give = sides[2 * du : 2 * du + 2]
        arrived = []
        got = swap_core(give)
        for dx in range(1, x_count):
            arrived.append(shift_x(keep[dx] + got[dx], dx))
        halves = call(
            functools.partial(applied_kernel, du, len(arrived)),
            [chip((half, var_dev))] + [chip((sample_dev, var_dev))] * du,
            [(part, vmem) for part in (keep, got, residual, diagonal, *arrived, *halves)],
        )
        exchanged.append(exchange(halves[0], du))
    applied_parts = own_rows(halves[1])
    applied_slots = gather_slots(*exchanged, applied_parts)
    routed_applied = deliver(applied_slots)
    partial, new_diagonal = call(
        functools.partial(first_kernel, x_count, scale),
        [chip(tile_shape), (shape(1, var_dev), vmem)],
        [
            (row_local, smem),
            (place, smem),
            (omega_tiles, hbm),
            (diagonal, vmem),
            (resid_rows, vmem),
            (applied_slots[0], vmem),
        ]
        + [(part, vmem) for part in applied_parts + routed_resid],
        [
            pltpu.VMEM((sample_all, var_dev), f32),
            pltpu.VMEM((blocks_dev, block_size, depth), bf16),
            tile_sem,
        ],
        estimate=cost(2 * depth * tile_elements, 16 * tile_elements),
    )
    (new_tiles,) = call(
        last_kernel,
        [(shape(*tile_shape), hbm)],
        [
            (row_local, smem),
            (is_diag, smem),
            (resid_left, vmem),
            (partial, vmem),
        ]
        + [(part, vmem) for part in routed_applied],
        [pltpu.VMEM(tile_shape, f32), tile_sem],
    )
    return new_tiles, new_diagonal.reshape(var_dev)


def solution(mesh):
    rows, cols = mesh.shape["rows"], mesh.shape["cols"]
    fine = Mesh(mesh.devices.reshape(rows // 4, 2, 2, cols // 2, 2), ROWS + COLS)
    placed = (
        P(COLS, ROWS),
        P(None, ROWS),
        P(ROWS + COLS, None, None),
        P(ROWS),
        P(),
        P(),
    )
    return jax.shard_map(
        per_device,
        mesh=fine,
        in_specs=placed,
        out_specs=(P(ROWS + COLS, None, None), P(ROWS)),
        check_vma=False,
    )
```

```python
import functools

import jax
import jax.numpy as jnp
from jax import lax
from jax.experimental import pallas as pl
from jax.experimental.pallas import tpu as pltpu
from jax.sharding import Mesh
from jax.sharding import PartitionSpec as P

step_size = 0.5
penalty = 0.02

ROWS = ("a", "u", "v")
COLS = ("x", "k")
PLANE = ("u", "v", "x")


def plane_order(x_count):
    steps = [(du, dv, dx) for du in range(2) for dv in range(2) for dx in range(x_count)]
    return sorted(steps[1:], key=lambda step: sum(part > 0 for part in step))


NT = (((1,), (1,)), ((), ()))
NN = (((1,), (0,)), ((), ()))


def dot(left, right, dims):
    return lax.dot_general(left, right, dims, preferred_element_type=jnp.float32)


def split(value, pieces):
    found = []
    for _ in range(pieces):
        piece = value.astype(jnp.bfloat16)
        found.append(piece)
        value = value - piece.astype(jnp.float32)
    return found


def table_kernel(sizes, place, tile_rows, tile_cols, after, row_local, is_diag, slot_index):
    x_count, blocks = sizes
    a, u, v, x, k = (place[at] for at in range(5))
    tile_dev = row_local.shape[0]

    def first_tile(u, v, x):
        return ((((a * 2 + u) * 2 + v) * x_count + x) * 2 + k) * tile_dev

    mine = first_tile(u, v, x)
    for at in range(tile_dev):
        row, col = tile_rows[mine + at], tile_cols[mine + at]
        row_local[at] = row - ((a * 2 + u) * 2 + v) * blocks
        is_diag[at] = jnp.where(row == col, 1, 0)
    a_count = tile_cols.shape[0] // (8 * x_count * tile_dev)
    peer = 0
    for du in range(2):
        for dv in range(2):
            for dx in range(x_count):
                theirs = first_tile(u ^ du, v ^ dv, lax.rem(x + dx, x_count))
                for at in range(tile_dev):
                    col = tile_cols[theirs + at]
                    group = col // blocks
                    da = lax.rem(a + a_count - group // 4, a_count)
                    part = (da * 2 + (((group // 2) % 2) ^ u)) * 2 + ((group % 2) ^ k)
                    slot_index[peer * tile_dev + at] = part * blocks + col % blocks
                peer += 1


def score_kernel(samples, loadings, out, held_samples, held, sem):
    rows, variables = samples.shape
    chunks = sem.shape[0] - 1
    width = variables // chunks
    whole = pltpu.make_async_copy(samples, held_samples, sem.at[chunks])
    whole.start()
    copies = [
        pltpu.make_async_copy(
            loadings.at[:, at * width : (at + 1) * width],
            held.at[:, at * width : (at + 1) * width],
            sem.at[at],
        )
        for at in range(chunks)
    ]
    for copy in copies:
        copy.start()
    whole.wait()
    found = None
    for at, copy in enumerate(copies):
        here = slice(at * width, (at + 1) * width)
        pieces = jnp.concatenate(split(held_samples[:, here], 3), 0)
        copy.wait()
        term = dot(pieces, held[:, here], NT)
        found = term if found is None else found + term
    value = (found[2 * rows :] + found[rows : 2 * rows]) + found[:rows]
    for copy in range(out.shape[0]):
        out[copy] = value


def residual_kernel(place, scores, samples, loadings, after, whole, first, second):
    rows, variables = samples.shape
    half = rows // 2
    value = scores[0]
    for source in range(1, scores.shape[0]):
        value = value + scores[source]
    pieces = jnp.concatenate(split(value, 3), 0)
    upper = place[1] == 1
    width = variables // 4
    for at in range(0, variables, width):
        here = slice(at, at + width)
        fitted = dot(pieces, loadings[:, here], NN)
        value = samples[:, here] - ((fitted[2 * rows :] + fitted[rows : 2 * rows]) + fitted[:rows])
        low, high = value[:half], value[half:]
        near = jnp.where(upper, high, low)
        far = jnp.where(upper, low, high)
        whole[:half, here] = near
        whole[half:, here] = far
        first[:, here] = near
        second[:, here] = far


def gather_kernel(count, peers, index, *refs):
    sources, outs, held = refs[:count], refs[-1 - peers : -1], refs[-1]
    for at, source in enumerate(sources):
        held[at] = source[...]
    tile_dev, _, width = outs[0].shape
    blocks = held.shape[2] // width
    for peer, out in enumerate(outs):
        for at in range(tile_dev):
            code = index[peer * tile_dev + at]
            start = pl.multiple_of((code % blocks) * width, width)
            out[at] = held[code // blocks, :, pl.ds(start, width)]


def block_of(routed, at):
    return jnp.concatenate([part[at] for part in routed], 0)


def masked(tile, is_diag):
    size = tile.shape[0]
    row = lax.broadcasted_iota(jnp.int32, (size, size), 0)
    col = lax.broadcasted_iota(jnp.int32, (size, size), 1)
    return jnp.where((row == col) & (is_diag == 1), 0.0, tile)


def fetch_tiles(tiles, held, sem):
    copies = [
        pltpu.make_async_copy(tiles.at[at], held.at[at], sem.at[at]) for at in range(tiles.shape[0])
    ]
    for copy in copies:
        copy.start()


def tile_kernel(is_diag, tiles, after, high, low, held, sem):
    fetch_tiles(tiles, held, sem)

    def convert(at, carry):
        pltpu.make_async_copy(tiles.at[at], held.at[at], sem.at[at]).wait()
        high[at], low[at] = split(masked(held[at], is_diag[at]), 2)
        return carry

    lax.fori_loop(0, tiles.shape[0], convert, 0)


def product_kernel(x_count, row_local, place, tile_hi, tile_lo, after, *refs):
    routed, sides, total = refs[:-5], refs[-5:-1], refs[-1]
    blocks, samples, block = total.shape
    total[...] = jnp.zeros_like(total)

    def multiply(at, carry):
        source_hi, source_lo = split(block_of(routed, at), 2)
        stacked = dot(jnp.concatenate([source_hi, source_lo], 0), tile_hi[at], NT)
        product = stacked[:samples] + (stacked[samples:] + dot(source_hi, tile_lo[at], NT))
        total[row_local[at]] += product
        return carry

    lax.fori_loop(0, tile_hi.shape[0], multiply, 0)
    for side, out in enumerate(sides):
        du, core = side // 2, place[4] ^ (side % 2)
        half = out.shape[1]
        for dx in range(x_count):
            source = (du * 2 + (place[2] ^ core)) * x_count + (x_count - dx) % x_count
            start = pl.multiple_of(source * half, half)
            for at in range(blocks):
                out[dx, :, at * block : (at + 1) * block] = total[at, pl.ds(start, half), :]


def applied_kernel(du, count, *refs):
    keep, got, residual, diagonal = refs[:4]
    arrived = refs[4 : 4 + count]
    half = keep.shape[1]
    value = keep[0] + got[0]
    for other in arrived:
        value = value + other[...]
    value = value + diagonal[...] * residual[du * half : (du + 1) * half]
    if du == 0:
        refs[-1][...] = value
    else:
        earlier, part, whole = refs[-3:]
        part[...] = value
        whole[:half] = earlier[...]
        whole[half:] = value


def place_rows(x_count, place, parts, rows):
    half = parts[0].shape[0] // 2
    for dk in range(2):
        for dx in range(x_count):
            for du in range(2):
                target = (du * 2 + (place[2] ^ place[4] ^ dk)) * x_count + dx
                start = pl.multiple_of(target * half, half)
                rows[pl.ds(start, half)] = parts[dk * x_count + dx][du * half : (du + 1) * half]


def left_operand(rows, scale):
    high, low = split((rows * scale).T, 2)
    return jnp.concatenate([high, high, low], 1)


def right_operand(rows):
    high, low = split(rows, 2)
    return jnp.concatenate([high, low, high], 0)


def row_kernel(x_count, scale, place, after, *refs):
    parts, (rows, left) = refs[:-2], refs[-2:]
    place_rows(x_count, place, parts, rows)
    block = left.shape[1]
    for at in range(left.shape[0]):
        left[at] = left_operand(rows[:, at * block : (at + 1) * block], scale)


def first_kernel(x_count, scale, row_local, place, tiles, diagonal, resid_rows, after, *refs):
    inputs, (partial, new_diagonal, rows, left, sem) = refs[:-5], refs[-5:]
    parts, routed = inputs[: 2 * x_count], inputs[2 * x_count :]
    fetch_tiles(tiles, partial, sem)
    samples = rows.shape[0]
    block = left.shape[1]
    place_rows(x_count, place, parts, rows)
    for at in range(left.shape[0]):
        left[at] = left_operand(rows[:, at * block : (at + 1) * block], scale)
    stat = jnp.sum(rows[...] * resid_rows[...], axis=0, keepdims=True) / samples
    new_diagonal[...] = diagonal[...] - step_size * (stat - 1.0 / diagonal[...])

    def subtract(at, carry):
        right = right_operand(block_of(routed, at))
        term = dot(left[row_local[at]], right, NN)
        pltpu.make_async_copy(tiles.at[at], partial.at[at], sem.at[at]).wait()
        partial[at] = partial[at] + term
        return carry

    lax.fori_loop(0, tiles.shape[0], subtract, 0)


def last_kernel(row_local, is_diag, left, partial, *refs):
    routed, (new_tiles, held, sem) = refs[:-3], refs[-3:]
    bound = step_size * penalty

    def finish(at, carry):
        right = right_operand(block_of(routed, at))
        stepped = partial[at] + dot(left[row_local[at]], right, NN)
        held[at] = stepped - jnp.clip(stepped, -bound, bound)

        @pl.when(is_diag[at] == 1)
        def _():
            held[at] = masked(held[at], 1)

        pltpu.make_async_copy(held.at[at], new_tiles.at[at], sem.at[at]).start()
        return carry

    lax.fori_loop(0, partial.shape[0], finish, 0)
    for at in range(partial.shape[0]):
        pltpu.make_async_copy(held.at[at], new_tiles.at[at], sem.at[at]).wait()


def per_device(samples, loadings, omega_tiles, omega_diagonal, tile_rows, tile_cols):
    f32 = jnp.float32
    a_count, x_count = lax.axis_size("a"), lax.axis_size("x")
    row_count, col_count = 4 * a_count, 2 * x_count
    a, u, v, x, k = (lax.axis_index(name) for name in ROWS + COLS)
    sample_dev, var_dev = samples.shape
    half = sample_dev // 2
    sample_all = sample_dev * col_count
    factors = loadings.shape[0]
    tile_dev, block_size = omega_tiles.shape[:2]
    blocks_dev = var_dev // block_size
    plane = 4 * x_count
    hbm = pl.BlockSpec(memory_space=pltpu.HBM)
    vmem = pl.BlockSpec(memory_space=pltpu.VMEM)

    def cost(flops, moved):
        return pl.CostEstimate(flops=flops, bytes_accessed=moved, transcendentals=0)

    shape = lambda *dims: jax.ShapeDtypeStruct(dims, f32)

    place = jnp.stack([a, u, v, x, k]).astype(jnp.int32)

    def permute(value, names, target):
        sizes = [lax.axis_size(name) for name in names]

        def flat(coords):
            at = 0
            for coord, size in zip(coords, sizes):
                at = at * size + coord
            return at

        def coords_of(at):
            coords = []
            for size in reversed(sizes):
                coords.append(at % size)
                at //= size
            return tuple(reversed(coords))

        total = 1
        for size in sizes:
            total *= size
        return lax.ppermute(
            value, names, [(at, flat(target(*coords_of(at)))) for at in range(total)]
        )

    def swap_core(value):
        return permute(value, ("k",), lambda k: (1 - k,))

    def shift_x(value, dx):
        return permute(value, ("x",), lambda x: ((x + dx) % x_count,))

    def call(kernel, outs, operands, scratch=(), limit=24, estimate=None):
        arrays, specs = [], []
        for array, spec in operands:
            if spec is vmem:
                array = pltpu.with_memory_space_constraint(array, pltpu.VMEM)
            if spec is hbm:
                array = pltpu.with_memory_space_constraint(array, pltpu.HBM)
            arrays.append(array)
            specs.append(spec)
        return pl.pallas_call(
            kernel,
            out_shape=[out for out, _ in outs],
            in_specs=specs,
            out_specs=[spec for _, spec in outs],
            scratch_shapes=list(scratch),
            compiler_params=pltpu.CompilerParams(vmem_limit_bytes=limit * 1024 * 1024),
            cost_estimate=estimate,
        )(*arrays)

    def chip(dims, dtype=f32):
        return (pltpu.VMEM(dims, dtype), vmem)

    smem = pl.BlockSpec(memory_space=pltpu.SMEM)
    bf16 = jnp.bfloat16
    diagonal = omega_diagonal.reshape(1, var_dev)
    depth = 3 * sample_all
    tile_elements = tile_dev * block_size * block_size
    tile_sem = pltpu.SemaphoreType.DMA((tile_dev,))
    tile_shape = omega_tiles.shape
    scale = -step_size * 0.5 / sample_all
    field_outs = [chip((sample_dev, var_dev)), chip((half, var_dev)), chip((half, var_dev))]

    score_copies, held_samples, held_loadings = call(
        score_kernel,
        [
            chip((row_count, sample_dev, factors)),
            chip(samples.shape),
            chip(loadings.shape, bf16),
        ],
        [(samples, hbm), (loadings, hbm)],
        [pltpu.SemaphoreType.DMA((9,))],
    )
    score_terms = lax.all_to_all(score_copies, ROWS, 0, 0, tiled=True)
    row_local, is_diag, slot_index = call(
        functools.partial(table_kernel, (x_count, blocks_dev)),
        [
            (jax.ShapeDtypeStruct((count,), jnp.int32), smem)
            for count in (tile_dev, tile_dev, plane * tile_dev)
        ],
        [(place, smem), (tile_rows, smem), (tile_cols, smem), (score_copies, vmem)],
    )
    residual, resid_near, resid_far = call(
        residual_kernel,
        field_outs,
        [
            (place, smem),
            (score_terms, vmem),
            (held_samples, vmem),
            (held_loadings, vmem),
            (slot_index, smem),
        ],
    )

    def own_rows(whole):
        parts = [whole]
        for dx in range(1, x_count):
            parts.append(shift_x(whole, dx))
        return parts

    def both_cores(parts):
        swapped = []
        for part in parts:
            swapped.append(swap_core(part))
        return parts + swapped

    def exchange(part, dz):
        held = [None] * a_count
        for da in range(a_count):
            held[da] = permute(
                part,
                ("a", "u", "v", "k"),
                lambda a, u, v, k: ((a + da) % a_count, u ^ dz, k, v),
            )
        return [[arrived, swap_core(arrived)] for arrived in held]

    def gather_slots(near, far, beside):
        sources = [part for pair in zip(near, far) for parts in pair for part in parts]
        return call(
            functools.partial(gather_kernel, len(sources), plane),
            [chip((tile_dev, half, block_size))] * plane,
            [(slot_index, smem)] + [(part, vmem) for part in sources + beside],
            [pltpu.VMEM((len(sources), half, var_dev), f32)],
        )

    def deliver(slots):
        routed = list(slots)
        for du, dv, dx in plane_order(x_count):
            at = (du * 2 + dv) * x_count + dx
            routed[at] = permute(
                slots[at], PLANE, lambda u, v, x: (u ^ du, v ^ dv, (x + dx) % x_count)
            )
        return routed

    resid_parts = own_rows(residual)
    resid_slots = gather_slots(exchange(resid_near, 0), exchange(resid_far, 1), resid_parts)
    routed_resid = deliver(resid_slots)
    resid_parts = both_cores(resid_parts)
    tiles_hi, tiles_lo = call(
        tile_kernel,
        [chip(tile_shape, bf16), chip(tile_shape, bf16)],
        [(is_diag, smem), (omega_tiles, hbm), (resid_slots[0], vmem)],
        [pltpu.VMEM(tile_shape, f32), tile_sem],
        estimate=cost(0, 8 * tile_elements),
    )
    resid_rows, resid_left = call(
        functools.partial(row_kernel, x_count, scale),
        [chip((sample_all, var_dev)), chip((blocks_dev, block_size, depth), bf16)],
        [(place, smem), (resid_slots[0], vmem)] + [(part, vmem) for part in resid_parts],
        estimate=cost(0, 16 * sample_all * var_dev),
    )

    sides = call(
        functools.partial(product_kernel, x_count),
        [chip((x_count, half, var_dev))] * 4,
        [
            (row_local, smem),
            (place, smem),
            (tiles_hi, vmem),
            (tiles_lo, vmem),
            (resid_left, vmem),
        ]
        + [(part, vmem) for part in routed_resid],
        [pltpu.VMEM((blocks_dev, sample_all, block_size), f32)],
    )
    halves, exchanged = [], []
    for du in range(2):
        keep, give = sides[2 * du : 2 * du + 2]
        arrived = []
        got = swap_core(give)
        for dx in range(1, x_count):
            arrived.append(shift_x(keep[dx] + got[dx], dx))
        halves = call(
            functools.partial(applied_kernel, du, len(arrived)),
            [chip((half, var_dev))] + [chip((sample_dev, var_dev))] * du,
            [(part, vmem) for part in (keep, got, residual, diagonal, *arrived, *halves)],
        )
        exchanged.append(exchange(halves[0], du))
    applied_parts = own_rows(halves[1])
    applied_slots = gather_slots(*exchanged, applied_parts)
    routed_applied = deliver(applied_slots)
    applied_parts = both_cores(applied_parts)
    partial, new_diagonal = call(
        functools.partial(first_kernel, x_count, scale),
        [chip(tile_shape), (shape(1, var_dev), vmem)],
        [
            (row_local, smem),
            (place, smem),
            (omega_tiles, hbm),
            (diagonal, vmem),
            (resid_rows, vmem),
            (applied_slots[0], vmem),
        ]
        + [(part, vmem) for part in applied_parts + routed_resid],
        [
            pltpu.VMEM((sample_all, var_dev), f32),
            pltpu.VMEM((blocks_dev, block_size, depth), bf16),
            tile_sem,
        ],
        estimate=cost(2 * depth * tile_elements, 16 * tile_elements),
    )
    (new_tiles,) = call(
        last_kernel,
        [(shape(*tile_shape), hbm)],
        [
            (row_local, smem),
            (is_diag, smem),
            (resid_left, vmem),
            (partial, vmem),
        ]
        + [(part, vmem) for part in routed_applied],
        [pltpu.VMEM(tile_shape, f32), tile_sem],
    )
    return new_tiles, new_diagonal.reshape(var_dev)


def solution(mesh):
    rows, cols = mesh.shape["rows"], mesh.shape["cols"]
    fine = Mesh(mesh.devices.reshape(rows // 4, 2, 2, cols // 2, 2), ROWS + COLS)
    placed = (
        P(COLS, ROWS),
        P(None, ROWS),
        P(ROWS + COLS, None, None),
        P(ROWS),
        P(),
        P(),
    )
    return jax.shard_map(
        per_device,
        mesh=fine,
        in_specs=placed,
        out_specs=(P(ROWS + COLS, None, None), P(ROWS)),
        check_vma=False,
    )
```
